128 devices in a mesh: dp: 2 (over core), row: 4 (over x), col: 16 (over z, y).
Axes of the slice: x: 4, y: 4, z: 4, core: 2. Of those that a mesh axis runs over, the one named last changes fastest.
Arguments:
- forget_tokens: bfloat16 [256, 6144], P('dp', 'col'), may hold values from -6 to 6
- forget_cotangent: bfloat16 [256, 6144], P('dp', 'col'), may hold values from -6 to 6
- forget_labels: int32 [256], P('dp'), may hold values 0 or 1
- retain_tokens: bfloat16 [256, 6144], P('dp', 'col'), may hold values from -6 to 6
- ln_gain: float32 [6144], P('col'), may hold values from 0.25 to 1.75
- w_in: bfloat16 [6144, 24576], P('col', 'row'), may hold values from -0.078125 to 0.078125
- b_in: float32 [24576], P('row'), may hold values from -3 to 3
- w_out: bfloat16 [24576, 6144], P('row', 'col'), may hold values from -0.0390625 to 0.0390625
- b_out: float32 [6144], P('col'), may hold values from -3 to 3
- pruned: int32 [512], P('row'), may hold values from 0 to 24575, as said below
Outputs:
- saliency: float32 [24576], P('row')
- retain_out: bfloat16 [256, 6144], P(('dp', 'row'), 'col')
The draws below stay inside these ranges and needn't reach their ends.
Inputs may be any that keep to these rules, and one draw needn't show every extreme that they name: `pruned`: entries r * 128 to (r + 1) * 128 - 1 are distinct neurons that all lie in the r-th of the equal neuron ranges of the row shards.
All inputs are finite; a program needn't handle non-finite values. No bound on the sum of `forget_labels` on one device may be relied on, other than what follows from the above.
Results may differ from the reference program's by a relative error of at most 0.0052.
Values may be sent and summed in bfloat16 or wider, within the bound.
No kernel may reach another device: no remote copies, remote signals or barrier semaphores. Data moves between devices by JAX's collectives and lax.ppermute only.
A program may use at most 128 MiB of HBM per device.

```python
import jax
import jax.numpy as jnp
from jax import lax

D = 6144
FF = 24576
PR_DEV = 128
NF = 256
NR = 256
N_ROW = 4


def draw_pruned(key, part):
    width = FF // N_ROW

    def one_shard(shard):
        order = jax.random.permutation(jax.random.fold_in(key, shard), width)
        return order[:PR_DEV].astype(jnp.int32) + shard * width
    shards = jnp.arange(N_ROW, dtype=jnp.int32)
    return jax.vmap(one_shard)(shards).reshape(-1).astype(jnp.int32)


def set_ends(values, key, smallest, top_value):
    spot = [jax.random.randint(jax.random.fold_in(key, axis), (), 0, length) for axis, length in enumerate(values.shape)]
    longest = values.shape.index(max(values.shape))
    neighbour = spot[:longest] + [(spot[longest] + 1) % values.shape[longest]] + spot[longest + 1:]
    return values.at[tuple(spot)].set(smallest).at[tuple(neighbour)].set(top_value)


def level_of(own_key, shape, cuts, smallest, top_value):
    def one(dim, parts):
        steps = jax.random.uniform(jax.random.fold_in(jax.random.fold_in(own_key, 6), dim), (parts,), jnp.float32, smallest / len(cuts), top_value / len(cuts))
        return jnp.repeat(jnp.exp(steps), shape[dim] // parts).reshape((-1,) + (1,) * (len(shape) - dim - 1))

    loudness = one(*cuts[0])
    for cut in cuts[1:]:
        loudness = loudness * one(*cut)
    return loudness


def noise(own_key, dims, scale, most, cuts=(), kind=jnp.bfloat16):
    values = scale * jax.random.normal(own_key, dims, jnp.float32)
    if cuts:
        values = values * level_of(own_key, dims, cuts, -0.22, 0.18)
    return jnp.clip(values, -most, most).astype(kind)


def setup_inputs(seed: int = 0) -> dict:
    seeds = jax.random.split(jax.random.key(seed), 11)
    return {
        "forget_tokens": noise(seeds[0], (NF, D), 1.0, 6.0, ((0, 2), (1, 16))),
        "forget_cotangent": noise(seeds[1], (NF, D), 1.0, 6.0, ((0, 2), (1, 16))),
        "forget_labels": set_ends((jax.random.randint(seeds[2], (NF,), 0, 2) < 1).astype(jnp.int32), jax.random.fold_in(seeds[2], 1), 0, 1),
        "retain_tokens": noise(seeds[3], (NR, D), 1.0, 6.0, ((0, 2), (1, 16))),
        "ln_gain": jnp.clip(1.0 + 0.15 * jax.random.normal(seeds[4], (D,), jnp.float32), 0.25, 1.75),
        "w_in": noise(seeds[5], (D, FF), D ** -0.5, 0.078125, ((0, 16), (1, 4))),
        "b_in": noise(seeds[6], (FF,), 0.5, 3.0, ((0, 4),), jnp.float32),
        "w_out": noise(seeds[7], (FF, D), FF ** -0.5, 0.0390625, ((0, 4), (1, 16))),
        "b_out": noise(seeds[8], (D,), 0.5, 3.0, ((0, 16),), jnp.float32),
        "pruned": draw_pruned(jax.random.fold_in(seeds[10], 71), 0),
    }


def layer_norm(x, gain):
    xf = x.astype(jnp.float32)
    mean_val = lax.optimization_barrier(jnp.mean(xf, axis=1, keepdims=True))
    centred = xf - mean_val
    var_val = lax.optimization_barrier(jnp.mean(centred * centred, axis=1, keepdims=True))
    return (centred * lax.rsqrt(var_val + 1e-06) * gain).astype(jnp.bfloat16)

def gelu_exact(v):
    return v * 0.5 * (1.0 + lax.erf(v * 0.7071067811865476))

def gelu_slope(v):
    return 0.5 * (1.0 + lax.erf(v * 0.7071067811865476)) + v * jnp.exp(-0.5 * v * v) * 0.3989422804014327

def reference(forget_tokens, forget_cotangent, forget_labels, retain_tokens, ln_gain, w_in, b_in, w_out, b_out, pruned):
    normed_f = layer_norm(forget_tokens, ln_gain)
    normed_r = layer_norm(retain_tokens, ln_gain)
    pre_f = jnp.dot(normed_f, w_in, preferred_element_type=jnp.float32) + b_in
    pre_r = jnp.dot(normed_r, w_in, preferred_element_type=jnp.float32) + b_in
    act_f = gelu_exact(pre_f).astype(jnp.bfloat16)
    act_r = gelu_exact(pre_r).astype(jnp.bfloat16)
    grad_y = forget_cotangent * forget_labels[:, None].astype(jnp.bfloat16)
    grad_w_out = jnp.dot(act_f.T, grad_y, preferred_element_type=jnp.float32)
    grad_act = jnp.dot(grad_y, w_out.T, preferred_element_type=jnp.float32)
    grad_pre = (grad_act * gelu_slope(pre_f)).astype(jnp.bfloat16)
    grad_w_in = jnp.dot(normed_f.T, grad_pre, preferred_element_type=jnp.float32)
    term_in = lax.optimization_barrier(jnp.sum(jnp.abs(w_in.astype(jnp.float32) * grad_w_in), axis=0))
    term_out = lax.optimization_barrier(jnp.sum(jnp.abs(w_out.astype(jnp.float32) * grad_w_out), axis=1))
    saliency = (term_in + term_out) / D
    keep = jnp.ones((FF,), jnp.float32).at[pruned].set(0.0).astype(jnp.bfloat16)
    masked_r = act_r * keep[None, :]
    retain_out = (jnp.dot(masked_r, w_out, preferred_element_type=jnp.float32) + b_out).astype(jnp.bfloat16)
    return (saliency, retain_out)
```

```python
import jax
import jax.numpy as jnp
from jax import lax
from jax.sharding import PartitionSpec as P

D = 6144
SIDE = 4
BF16 = jnp.bfloat16
F32 = jnp.float32


def gelu_exact(v):
    return v * 0.5 * (1.0 + lax.erf(v * 0.7071067811865476))


def gelu_slope(v):
    return (
        0.5 * (1.0 + lax.erf(v * 0.7071067811865476))
        + v * jnp.exp(-0.5 * v * v) * 0.3989422804014327
    )


def shift_y(k):
    return [(z * 4 + y, z * 4 + (y + k) % 4) for z in range(4) for y in range(4)]


def shift_z(k):
    return [(z * 4 + y, ((z + k) % 4) * 4 + y) for z in range(4) for y in range(4)]


def shift_row(k):
    return [(r, (r + k) % 4) for r in range(4)]


SWAP = [(0, 1), (1, 0)]


def row_order(first, second):
    p = lax.broadcasted_iota(jnp.int32, (256, 256), 0)
    q = lax.broadcasted_iota(jnp.int32, (256, 256), 1)
    j, i, h, e = p // 64, (p // 16) % 4, (p // 8) % 2, p % 8
    src = h * 128 + (((first + j) % 4) * 4 + (second + i) % 4) * 8 + e
    return (src == q).astype(BF16)


def reorder(sel, x):
    return jnp.dot(sel, x, preferred_element_type=F32).astype(BF16)


def scatter_stage(parts, shift):
    got = [lax.ppermute(parts[j], "col", shift(j)) for j in (1, 2, 3)]
    return parts[0].astype(F32), [g.astype(F32) for g in got]


def scatter_sum(parts, first, second):
    rows = parts[0].shape[0] // 4
    got = [parts[0]] + [lax.ppermute(parts[j], "col", first(j)) for j in (1, 2, 3)]
    sums = []
    for i in range(4):
        own = got[0][i * rows : (i + 1) * rows].astype(F32)
        for j in (1, 2, 3):
            own = own + got[j][i * rows : (i + 1) * rows].astype(F32)
        sums.append(own)
    back = [lax.ppermute(sums[i].astype(BF16), "col", second(i)) for i in (1, 2, 3)]
    total = sums[0]
    for b in back:
        total = total + b.astype(F32)
    return total


def gather(block, first, second):
    group = jnp.concatenate(
        [block] + [lax.ppermute(block, "col", first(-i)) for i in (1, 2, 3)], axis=0
    )
    return [group] + [lax.ppermute(group, "col", second(-j)) for j in (1, 2, 3)]


def local(
    forget_tokens,
    forget_cotangent,
    forget_labels,
    retain_tokens,
    ln_gain,
    w_in,
    b_in,
    w_out,
    b_out,
    pruned,
):
    core = lax.axis_index("dp")
    row = lax.axis_index("row")
    col = lax.axis_index("col")
    y, z = col % 4, col // 4
    width = w_in.shape[0]
    half = w_in.shape[1] // 2

    grad_y_own = forget_cotangent * forget_labels[:, None].astype(BF16)
    own = jnp.concatenate([forget_tokens, retain_tokens, grad_y_own], axis=0)
    other = lax.ppermute(own, "dp", SWAP)

    x = own[:256].astype(F32)
    part_sum = jnp.sum(x, axis=1)
    centred = x - (part_sum / width)[:, None]
    part_m2 = jnp.sum(centred * centred, axis=1)
    stats = jnp.concatenate([part_sum, part_m2]).reshape(4, 128)
    stats = lax.all_to_all(
        jnp.broadcast_to(stats[None], (32, 4, 128)), ("dp", "col"), 0, 0, tiled=True
    )
    stats = stats.reshape(2, 16, 2, 256)
    sums, m2 = stats[:, :, 0], stats[:, :, 1]
    mean = jnp.sum(sums, axis=1) / D
    gap = sums / width - mean[:, None]
    var = (jnp.sum(m2, axis=1) + width * jnp.sum(gap * gap, axis=1)) / D
    scale = lax.rsqrt(var + 1e-06)

    def pick(v):
        mine = jnp.where(core == 0, v[0], v[1])
        theirs = jnp.where(core == 0, v[1], v[0])
        return mine[:, None], theirs[:, None]

    mean_own, mean_other = pick(mean)
    scale_own, scale_other = pick(scale)
    normed_own = ((x - mean_own) * scale_own * ln_gain).astype(BF16)
    normed_other = (
        (other[:256].astype(F32) - mean_other) * scale_other * ln_gain
    ).astype(BF16)

    sel_f = row_order(y, z)
    sel_r = row_order(z, y)
    grad_y = reorder(sel_f, jnp.concatenate([own[256:], other[256:]], axis=0))
    normed_f = reorder(sel_f, jnp.concatenate([normed_own[:128], normed_other[:128]], axis=0))
    normed_r = reorder(sel_r, jnp.concatenate([normed_own[128:], normed_other[128:]], axis=0))

    w_in_half = lax.dynamic_slice_in_dim(w_in, core * half, half, 1)
    w_out_half = lax.dynamic_slice_in_dim(w_out, core * half, half, 0)
    b_half = lax.dynamic_slice_in_dim(b_in, core * half, half, 0)

    grad_part = lax.dot_general(
        grad_y, w_out_half, (((1,), (1,)), ((), ())), preferred_element_type=F32
    ).astype(BF16)
    grad_act = scatter_sum([grad_part[j * 64 : (j + 1) * 64] for j in range(4)], shift_y, shift_z)
    part_f = jnp.dot(normed_f, w_in_half, preferred_element_type=F32).astype(BF16)
    pre_f = scatter_sum([part_f[j * 64 : (j + 1) * 64] for j in range(4)], shift_y, shift_z)
    part_r = jnp.dot(normed_r, w_in_half, preferred_element_type=F32).astype(BF16)
    pre_r = scatter_sum([part_r[j * 64 : (j + 1) * 64] for j in range(4)], shift_z, shift_y)

    pre_f = pre_f + b_half
    pre_r = pre_r + b_half
    act_f = gelu_exact(pre_f).astype(BF16)
    grad_pre = (grad_act * gelu_slope(pre_f)).astype(BF16)
    ids = row * w_in.shape[1] + core * half + jnp.arange(half, dtype=jnp.int32)
    is_pruned = jnp.any(pruned[:, None] == ids[None, :], axis=0)
    keep = jnp.where(is_pruned, 0.0, 1.0).astype(BF16)
    masked_r = gelu_exact(pre_r).astype(BF16) * keep[None, :]

    both = gather(jnp.concatenate([act_f, grad_pre], axis=0), shift_z, shift_y)
    both = jnp.concatenate(both, axis=0).reshape(4, 4, 2, 16, half)
    act_f = both[:, :, 0].reshape(256, half)
    grad_pre = both[:, :, 1].reshape(256, half)
    masked_r = jnp.concatenate(gather(masked_r, shift_y, shift_z), axis=0)

    def outer_rows(left, right):
        return lax.dot_general(
            left, right, (((0,), (0,)), ((), ())), preferred_element_type=F32
        )

    grad_w_in = outer_rows(normed_f, grad_pre)
    grad_w_out = outer_rows(act_f, grad_y)
    terms = jnp.sum(jnp.abs(w_in_half.astype(F32) * grad_w_in), axis=0) + jnp.sum(
        jnp.abs(w_out_half.astype(F32) * grad_w_out), axis=1
    )
    terms = jnp.broadcast_to(terms.reshape(1, half // 128, 128), (32, half // 128, 128))
    terms = lax.all_to_all(terms, ("dp", "col"), 0, 0, tiled=True)
    saliency = jnp.sum(terms.reshape(2, 16, half), axis=1).reshape(2 * half) / D

    out_part = jnp.dot(masked_r, w_out_half, preferred_element_type=F32)
    out_part = out_part.reshape(4, 4, 2, 8, width)
    mine = out_part[:, :, 0] + lax.ppermute(out_part[:, :, 1], "dp", SWAP)

    def for_row(r):
        return lax.dynamic_index_in_dim(mine, (r - z) % 4, 0, keepdims=False)

    total = for_row(row)
    for k in (1, 2, 3):
        total = total + lax.ppermute(for_row(row + k), "row", shift_row(k))
    retain_out = (total + b_out).astype(BF16)
    retain_out = lax.dynamic_slice_in_dim(
        jnp.concatenate([retain_out, retain_out], axis=0), (4 - y) % 4, 4, 0
    ).reshape(32, width)
    return (saliency, retain_out)


def solution(mesh):
    in_specs = (
        P("dp", "col"),
        P("dp", "col"),
        P("dp"),
        P("dp", "col"),
        P("col"),
        P("col", "row"),
        P("row"),
        P("row", "col"),
        P("col"),
        P("row"),
    )
    out_specs = (P("row"), P(("dp", "row"), "col"))
    return jax.shard_map(local, mesh=mesh, in_specs=in_specs, out_specs=out_specs, check_vma=False)
```

```python
import functools

import jax
import jax.numpy as jnp
from jax import lax
from jax.experimental import pallas as pl
from jax.experimental.pallas import tpu as pltpu
from jax.sharding import PartitionSpec as P

D = 6144
BF16 = jnp.bfloat16
F32 = jnp.float32
TILE = 512


def gelu_exact(v):
    return v * 0.5 * (1.0 + lax.erf(v * 0.7071067811865476))


def gelu_slope(v):
    return (
        0.5 * (1.0 + lax.erf(v * 0.7071067811865476))
        + v * jnp.exp(-0.5 * v * v) * 0.3989422804014327
    )


def shift_y(k):
    return [(z * 4 + y, z * 4 + (y + k) % 4) for z in range(4) for y in range(4)]


def shift_z(k):
    return [(z * 4 + y, ((z + k) % 4) * 4 + y) for z in range(4) for y in range(4)]


def shift_row(k):
    return [(r, (r + k) % 4) for r in range(4)]


SWAP = [(0, 1), (1, 0)]


def row_order(first, second):
    p = lax.broadcasted_iota(jnp.int32, (256, 256), 0)
    q = lax.broadcasted_iota(jnp.int32, (256, 256), 1)
    j, i = p >> 6, (p >> 4) & 3
    h, e = (p >> 3) & 1, p & 7
    src = h * 128 + (((first + j) & 3) * 4 + ((second + i) & 3)) * 8 + e
    return jnp.where(src == q, 1.0, 0.0).astype(BF16)


def reorder(sel, x):
    return jnp.dot(sel, x, preferred_element_type=F32).astype(BF16)


def centred_rows(own, other, gain):
    x = jnp.concatenate([own, other], axis=0).astype(F32)
    mean = jnp.sum(x, axis=1, keepdims=True) / x.shape[1]
    return ((x - mean) * gain).astype(BF16)


def forget_partials(where, own_x, other_x, own_g, other_g, gain, w_in, w_out, *rest):
    outs, (lhs_x, lhs_g) = rest[:4], rest[4:]

    @pl.when(pl.program_id(0) == 0)
    def _():
        sel = row_order(where[1], where[2])
        lhs_x[...] = reorder(sel, centred_rows(own_x[...], other_x[...], gain[...]))
        lhs_g[...] = reorder(sel, jnp.concatenate([own_g[...], other_g[...]], axis=0))

    pre = jnp.dot(lhs_x[...], w_in[...], preferred_element_type=F32).astype(BF16)
    grad = lax.dot_general(
        lhs_g[...], w_out[...], (((1,), (1,)), ((), ())), preferred_element_type=F32
    ).astype(BF16)
    for j in range(4):
        for i in range(4):
            at = (j * 4 + i) * 16
            outs[j][i * 32 : i * 32 + 16, :] = pre[at : at + 16]
            outs[j][i * 32 + 16 : i * 32 + 32, :] = grad[at : at + 16]


def retain_partials(where, own_x, other_x, gain, w_in, *rest):
    outs, g_out, lhs_x, lhs_gain = rest[:4], rest[4], rest[5], rest[6]

    @pl.when(pl.program_id(0) == 0)
    def _():
        sel = row_order(where[2], where[1])
        lhs_x[...] = reorder(sel, centred_rows(own_x[...], other_x[...], gain[...]))
        g0 = jnp.broadcast_to(gain[...], (16, gain.shape[1]))
        a = g0.astype(BF16)
        b = (g0 - a.astype(F32)).astype(BF16)
        c = (g0 - a.astype(F32) - b.astype(F32)).astype(BF16)
        lhs_gain[0:16, :] = a
        lhs_gain[16:32, :] = b
        lhs_gain[32:48, :] = c

    pre = jnp.dot(lhs_x[...], w_in[...], preferred_element_type=F32).astype(BF16)
    for j in range(4):
        outs[j][...] = pre[j * 64 : (j + 1) * 64]
    g = jnp.dot(lhs_gain[...], w_in[...], preferred_element_type=F32)
    g_out[...] = (g[32:40] + g[16:24]) + g[0:8]


def stage_sum(own, a, b, c, keep, *sends):
    rows = keep.shape[0]
    for i in range(4):
        at = slice(i * rows, (i + 1) * rows)
        total = (own[at, :].astype(F32) + a[at, :].astype(F32)) + (
            b[at, :].astype(F32) + c[at, :].astype(F32)
        )
        if i == 0:
            keep[...] = total
        else:
            sends[i - 1][...] = total.astype(BF16)


def preact(total, scale, gap, g_all, bias):
    corr = gap[:, 0:1] * g_all[0:1, :]
    for s in range(1, 16):
        corr = corr + gap[:, s : s + 1] * g_all[s : s + 1, :]
    return scale * (total + corr) + bias


def forget_act(keep, a, b, c, scale, gap, g_all, bias, out):
    total = (keep[...] + a[...].astype(F32)) + (b[...].astype(F32) + c[...].astype(F32))
    pre = preact(total[:16], scale[...], gap[...], g_all[...], bias[...])
    out[0:16, :] = gelu_exact(pre).astype(BF16)
    out[16:32, :] = (total[16:32] * gelu_slope(pre)).astype(BF16)


def retain_act(keep, a, b, c, scale, gap, g_all, bias, mask, out):
    total = (keep[...] + a[...].astype(F32)) + (b[...].astype(F32) + c[...].astype(F32))
    pre = preact(total, scale[...], gap[...], g_all[...], bias[...])
    out[...] = (gelu_exact(pre) * mask[...]).astype(BF16)


def saliency_terms(where, b0, b1, b2, b3, normed_t, grad_y, w_in, w_out, out):
    blocks = [b[i * 32 : i * 32 + 32, :] for b in (b0, b1, b2, b3) for i in range(4)]
    act = jnp.concatenate([b[:16] for b in blocks], axis=0)
    grad_pre = jnp.concatenate([b[16:] for b in blocks], axis=0)
    grad_in = jnp.dot(normed_t[...], grad_pre, preferred_element_type=F32)
    grad_out = lax.dot_general(
        act, grad_y[...], (((0,), (0,)), ((), ())), preferred_element_type=F32
    )
    term_in = jnp.sum(jnp.abs(w_in[...].astype(F32) * grad_in), axis=0, keepdims=True)
    prod = jnp.abs(w_out[...].astype(F32) * grad_out)
    lanes = (prod[:, 0:128] + prod[:, 128:256]) + prod[:, 256:384]
    term_out = jnp.sum(jnp.transpose(lanes), axis=0, keepdims=True)
    out[...] = term_in + term_out


def retain_product(where, b0, b1, b2, b3, w_out, out0, out1, acc):
    t = pl.program_id(0)
    act = jnp.concatenate([b0[...], b1[...], b2[...], b3[...]], axis=0)
    part = jnp.dot(act, w_out[...], preferred_element_type=F32)

    @pl.when(t == 0)
    def _():
        acc[...] = part

    @pl.when(t > 0)
    def _():
        acc[...] += part

    @pl.when(t == pl.num_programs(0) - 1)
    def _():
        for k in range(16):
            out0[k * 8 : k * 8 + 8, :] = acc[k * 16 : k * 16 + 8, :]
            out1[k * 8 : k * 8 + 8, :] = acc[k * 16 + 8 : k * 16 + 16, :]


def call(kernel, where, args, outs, scratch=(), steps=6, flops=0):
    def spec(shape, block, index):
        if block is None:
            return pl.BlockSpec(shape, lambda t, w: (0,) * len(shape))
        return pl.BlockSpec(block, index)

    size = sum(a.size * a.dtype.itemsize for a, _, _ in args)
    return pl.pallas_call(
        kernel,
        grid_spec=pltpu.PrefetchScalarGridSpec(
            num_scalar_prefetch=1,
            grid=(steps,),
            in_specs=[spec(a.shape, b, i) for a, b, i in args],
            out_specs=[spec(s, b, i) for s, _, b, i in outs],
            scratch_shapes=list(scratch),
        ),
        out_shape=[jax.ShapeDtypeStruct(s, d) for s, d, _, _ in outs],
        compiler_params=pltpu.CompilerParams(vmem_limit_bytes=40 * 2**20),
        cost_estimate=pl.CostEstimate(flops=flops, bytes_accessed=size, transcendentals=0),
    )(where, *[a for a, _, _ in args])


def whole(a):
    return (a, None, None)


def by_n(a, tile=TILE):
    return (a, (a.shape[0], tile), lambda t, w: (0, t))


def out_n(rows, n, dtype, tile=TILE):
    return ((rows, n), dtype, (rows, tile), lambda t, w: (0, t))


def drop_where(kernel):
    def inner(where, *refs):
        kernel(*refs)

    return inner


def permutes(parts, shift, sign=1):
    return [lax.ppermute(parts[k], "col", shift(sign * (k + 1))) for k in range(3)]


def after(value, *others):
    return lax.optimization_barrier((value, *others))[0]


def local(
    forget_tokens,
    forget_cotangent,
    forget_labels,
    retain_tokens,
    ln_gain,
    w_in,
    b_in,
    w_out,
    b_out,
    pruned,
):
    core = lax.axis_index("dp")
    row = lax.axis_index("row")
    col = lax.axis_index("col")
    y, z = col % 4, col // 4
    width = w_in.shape[0]
    half = w_in.shape[1] // 2
    steps = half // TILE
    where = jnp.stack([core, y, z]).astype(jnp.int32)
    gain = ln_gain[None, :]

    own_g = forget_cotangent * forget_labels[:, None].astype(BF16)
    own = jnp.concatenate([forget_tokens, own_g, retain_tokens], axis=0)
    other = lax.ppermute(own, "dp", SWAP)

    def rows_of(k):
        return lambda t, w: (k, 0)

    def third(a, k):
        return (a, (128, width), rows_of(k))

    w_in_tile = (w_in, (width, TILE), lambda t, w: (0, w[0] * steps + t))
    w_out_tile = (w_out, (TILE, width), lambda t, w: (w[0] * steps + t, 0))

    f_parts = call(
        forget_partials,
        where,
        [third(own, 0), third(other, 0), third(own, 1), third(other, 1), whole(gain),
         w_in_tile, w_out_tile],
        [out_n(128, half, BF16)] * 4,
        [pltpu.VMEM((256, width), BF16)] * 2,
        steps,
        4 * 256 * width * half,
    )
    f_got = permutes(f_parts[1:], shift_y)
    own_r, _ = lax.optimization_barrier((own, f_parts[0]))
    r_parts = call(
        retain_partials,
        where,
        [third(own_r, 2), third(other, 2), whole(gain), w_in_tile],
        [out_n(64, half, BF16)] * 4 + [out_n(8, half, F32)],
        [pltpu.VMEM((256, width), BF16), pltpu.VMEM((48, width), BF16)],
        steps,
        2 * 256 * width * half,
    )
    g_part = r_parts[4]
    r_got = permutes(r_parts[1:4], shift_z)

    own_s, other_s, _ = lax.optimization_barrier((own, other, r_parts[0]))
    tokens = jnp.stack([own_s, other_s]).reshape(2, 3, 128, width)[:, ::2].astype(F32)
    part_mean = jnp.sum(tokens, axis=3) / width
    centred = tokens - part_mean[..., None]
    part_m2 = jnp.sum(centred * centred, axis=3)
    share = jnp.concatenate(
        [part_mean.reshape(4, 128), part_m2.reshape(4, 128), g_part[0].reshape(half // 128, 128)]
    )
    share = lax.all_to_all(
        jnp.broadcast_to(share[None], (16,) + share.shape), "col", 0, 0, tiled=True
    )
    means = share[:, 0:4].reshape(16, 2, 2, 128)
    m2 = share[:, 4:8].reshape(16, 2, 2, 128)
    g_all = share[:, 8:].reshape(16, half)
    mean = jnp.mean(means, axis=0)
    gap = means - mean
    var = (jnp.sum(m2, axis=0) + width * jnp.sum(gap * gap, axis=0)) / D
    scale = lax.rsqrt(var + 1e-06)

    def owned(v, block):
        v = v.reshape(v.shape[:-1] + (16, 8))
        return lax.dynamic_index_in_dim(v, block, v.ndim - 2, False).reshape(
            v.shape[:-3] + (16,)
        )

    f_scale, f_gap = owned(scale[:, 0], y * 4 + z)[:, None], owned(gap[:, :, 0], y * 4 + z).T
    r_scale, r_gap = owned(scale[:, 1], z * 4 + y)[:, None], owned(gap[:, :, 1], z * 4 + y).T

    b_half = lax.dynamic_slice_in_dim(b_in, core * half, half, 0)[None, :]
    ids = row * w_in.shape[1] + core * half + jnp.arange(half, dtype=jnp.int32)
    is_pruned = jnp.any(pruned[:, None] == ids[None, :], axis=0)
    keep = jnp.where(is_pruned, 0.0, 1.0)[None, :]

    sel_f = row_order(y, z)
    tok = jnp.concatenate([own_s[:128], other_s[:128]], axis=0).astype(F32)
    normed_f = (tok - mean[:, 0].reshape(256, 1)) * scale[:, 0].reshape(256, 1) * gain
    normed_f = reorder(sel_f, normed_f.astype(BF16))
    grad_y = reorder(sel_f, jnp.concatenate([own_s[128:256], other_s[128:256]], axis=0))
    normed_t = normed_f.T

    f_sums = call(
        drop_where(stage_sum),
        where,
        [by_n(a, 1024) for a in [f_parts[0]] + f_got],
        [out_n(32, half, F32, 1024)] + [out_n(32, half, BF16, 1024)] * 3,
        steps=half // 1024,
    )
    f_back = permutes(f_sums[1:], shift_z)
    r_sums = call(
        drop_where(stage_sum),
        where,
        [by_n(a, 1024) for a in [r_parts[0]] + r_got],
        [out_n(16, half, F32, 1024)] + [out_n(16, half, BF16, 1024)] * 3,
        steps=half // 1024,
    )
    r_back = permutes(r_sums[1:], shift_y)

    f_block = call(
        drop_where(forget_act),
        where,
        [by_n(a, 1024) for a in [f_sums[0]] + f_back]
        + [whole(f_scale), whole(f_gap), by_n(g_all, 1024), by_n(b_half, 1024)],
        [out_n(32, half, BF16, 1024)],
        steps=half // 1024,
    )[0]
    f_group = jnp.concatenate([f_block] + permutes([f_block] * 3, shift_z, -1), axis=0)
    f_groups = [f_group] + permutes([f_group] * 3, shift_y, -1)
    r_block = call(
        drop_where(retain_act),
        where,
        [by_n(a, 1024) for a in [r_sums[0]] + r_back]
        + [whole(r_scale), whole(r_gap), by_n(g_all, 1024), by_n(b_half, 1024), by_n(keep, 1024)],
        [out_n(16, half, BF16, 1024)],
        steps=half // 1024,
    )[0]
    r_group = jnp.concatenate([r_block] + permutes([r_block] * 3, shift_y, -1), axis=0)
    r_groups = [r_group] + permutes([r_group] * 3, shift_z, -1)

    terms = call(
        saliency_terms,
        where,
        [by_n(a) for a in f_groups] + [whole(normed_t), whole(grad_y), w_in_tile, w_out_tile],
        [out_n(1, half, F32)],
        (),
        steps,
        4 * 256 * width * half,
    )[0]
    terms = jnp.broadcast_to(terms.reshape(1, half // 128, 128), (32, half // 128, 128))
    terms = lax.all_to_all(terms, ("dp", "col"), 0, 0, tiled=True)
    saliency = jnp.sum(terms.reshape(2, 16, half), axis=1).reshape(2 * half) / D

    mine, theirs = call(
        retain_product,
        where,
        [by_n(a) for a in r_groups] + [w_out_tile],
        [((128, width), F32, None, None)] * 2,
        [pltpu.VMEM((256, width), F32)],
        steps,
        2 * 256 * width * half,
    )
    mine = (mine + lax.ppermute(theirs, "dp", SWAP)).reshape(4, 4, 8, width)

    def for_row(r):
        return lax.dynamic_index_in_dim(mine, (r - z) % 4, 0, keepdims=False)

    total = for_row(row)
    for k in (1, 2, 3):
        total = total + lax.ppermute(for_row(row + k), "row", shift_row(k))
    retain_out = (total + b_out).astype(BF16)
    retain_out = lax.dynamic_slice_in_dim(
        jnp.concatenate([retain_out, retain_out], axis=0), (4 - y) % 4, 4, 0
    ).reshape(32, width)
    return (saliency, retain_out)


def solution(mesh):
    in_specs = (
        P("dp", "col"),
        P("dp", "col"),
        P("dp"),
        P("dp", "col"),
        P("col"),
        P("col", "row"),
        P("row"),
        P("row", "col"),
        P("col"),
        P("row"),
    )
    out_specs = (P("row"), P(("dp", "row"), "col"))
    return jax.shard_map(local, mesh=mesh, in_specs=in_specs, out_specs=out_specs, check_vma=False)
```

```python
import functools

import jax
import jax.numpy as jnp
from jax import lax
from jax.experimental import pallas as pl
from jax.experimental.pallas import tpu as pltpu
from jax.sharding import PartitionSpec as P

D = 6144
BF16 = jnp.bfloat16
F32 = jnp.float32
TILE = 512
WIDE = 1024


def gelu_exact(v):
    return v * 0.5 * (1.0 + lax.erf(v * 0.7071067811865476))


def gelu_slope(v):
    return (
        0.5 * (1.0 + lax.erf(v * 0.7071067811865476))
        + v * jnp.exp(-0.5 * v * v) * 0.3989422804014327
    )


def shift_y(k):
    return [(z * 4 + y, z * 4 + (y + k) % 4) for z in range(4) for y in range(4)]


def shift_z(k):
    return [(z * 4 + y, ((z + k) % 4) * 4 + y) for z in range(4) for y in range(4)]


def shift_row(k):
    return [(r, (r + k) % 4) for r in range(4)]


SWAP = [(0, 1), (1, 0)]


def row_order(where, swap, kinds):
    size = 128 * kinds
    bit = kinds - 1
    p = lax.broadcasted_iota(jnp.int32, (size, size), 0)
    q = lax.broadcasted_iota(jnp.int32, (size, size), 1)
    e, h, b = p & 7, (p >> 3) & bit, p >> (3 + bit)
    j, i = b >> 2, b & 3
    by, bz = (i, j) if swap else (j, i)
    block = ((where[1] + by) & 3) * 4 + ((where[2] + bz) & 3)
    return jnp.where(h * 128 + block * 8 + e == q, 1.0, 0.0).astype(BF16)


def reorder(sel, x):
    return jnp.dot(sel, x, preferred_element_type=F32).astype(BF16)


def partials(swap, where, x_f, x_g, x_r, gain, w_in, w_out, *rest):
    outs, g_rows, rest = rest[:4], rest[4], rest[5:]
    lhs_x = rest[-1]
    if swap:
        g_out, lhs_gain = rest[0], rest[1]

    @pl.when(pl.program_id(0) == 0)
    def _():
        x = jnp.concatenate([x_f[...], x_r[...]], axis=0).astype(F32)
        mean = jnp.sum(x, axis=1, keepdims=True) / x.shape[1]
        x = ((x - mean) * gain[...]).astype(BF16)
        lhs_x[...] = reorder(row_order(where, swap, 2), x)
        g_rows[...] = reorder(row_order(where, swap, 1), x_g[...])
        if swap:
            g0 = jnp.broadcast_to(gain[...], (16, gain.shape[1]))
            a = g0.astype(BF16)
            b = (g0 - a.astype(F32)).astype(BF16)
            c = (g0 - a.astype(F32) - b.astype(F32)).astype(BF16)
            lhs_gain[0:16, :] = a
            lhs_gain[16:32, :] = b
            lhs_gain[32:48, :] = c

    pre = jnp.dot(lhs_x[...], w_in[...], preferred_element_type=F32)
    grad = lax.dot_general(
        g_rows[...], w_out[...], (((1,), (1,)), ((), ())), preferred_element_type=F32
    )
    for j in range(4):
        rows = []
        for i in range(4):
            at = j * 4 + i
            rows += [pre[at * 16 : at * 16 + 16], grad[at * 8 : at * 8 + 8]]
        outs[j][...] = jnp.concatenate(rows, axis=0).astype(BF16)
    if swap:
        g = jnp.dot(lhs_gain[...], w_in[...], preferred_element_type=F32)
        g_out[...] = (g[32:40] + g[16:24]) + g[0:8]


def stage_sum(own, a, b, c, keep, *sends):
    rows = keep.shape[0]
    total = (own[...].astype(F32) + a[...].astype(F32)) + (
        b[...].astype(F32) + c[...].astype(F32)
    )
    keep[...] = total[:rows]
    for i in (1, 2, 3):
        sends[i - 1][...] = total[i * rows : (i + 1) * rows].astype(BF16)


def activate(width, keep, a, b, c, means, m2, g_all, bias, mask, out):
    total = (keep[...] + a[...].astype(F32)) + (b[...].astype(F32) + c[...].astype(F32))
    m = means[...]
    gap = m - jnp.sum(m, axis=1, keepdims=True) / 16
    var = (
        jnp.sum(m2[...], axis=1, keepdims=True)
        + width * jnp.sum(gap * gap, axis=1, keepdims=True)
    ) / D
    pre = total[:16]
    for s in range(16):
        pre = pre + gap[:, s : s + 1] * g_all[s : s + 1, :]
    pre = lax.rsqrt(var + 1e-06) * pre + bias[...]
    act = gelu_exact(pre)
    act_r = act[8:16].astype(BF16).astype(F32) * mask[...]
    grad_pre = total[16:24] * gelu_slope(pre[:8])
    out[...] = jnp.concatenate([act[:8], act_r, grad_pre], axis=0).astype(BF16)


def regroup(b0, b1, b2, b3, forget, retain):
    blocks = [b[...].astype(F32) for b in (b0, b1, b2, b3)]
    forget[...] = jnp.concatenate(
        [b[0:8] for b in blocks] + [b[16:24] for b in blocks], axis=0
    ).astype(BF16)
    retain[...] = jnp.concatenate([b[8:16] for b in blocks], axis=0).astype(BF16)


def normalise(width, where, x_own, x_other, means, m2, gain, out):
    for k, x in enumerate((x_own, x_other)):
        m, q = means[k * 128 : k * 128 + 128, :], m2[k * 128 : k * 128 + 128, :]
        mean = jnp.sum(m, axis=1, keepdims=True) / 16
        gap = m - mean
        var = (
            jnp.sum(q, axis=1, keepdims=True) + width * jnp.sum(gap * gap, axis=1, keepdims=True)
        ) / D
        normed = ((x[...].astype(F32) - mean) * lax.rsqrt(var + 1e-06) * gain[...]).astype(BF16)
        rows = jnp.dot(row_order(where, k == 1, 1), normed, preferred_element_type=F32)
        out[:, k * 128 : k * 128 + 128] = jnp.transpose(rows).astype(BF16)


def saliency_terms(where, *refs):
    blocks, (normed_t, g_own, g_other, w_in, w_out, out) = refs[:8], refs[8:]
    act = jnp.concatenate([b[0:32, :] for b in blocks], axis=0)
    grad_pre = jnp.concatenate([b[32:64, :] for b in blocks], axis=0)
    grad_y = jnp.concatenate([g_own[...], g_other[...]], axis=0)
    grad_in = jnp.dot(normed_t[...], grad_pre, preferred_element_type=F32)
    grad_out = lax.dot_general(
        act, grad_y, (((0,), (0,)), ((), ())), preferred_element_type=F32
    )
    term_in = jnp.sum(jnp.abs(w_in[...].astype(F32) * grad_in), axis=0, keepdims=True)
    prod = jnp.abs(w_out[...].astype(F32) * grad_out)
    lanes = (prod[:, 0:128] + prod[:, 128:256]) + prod[:, 256:384]
    term_out = jnp.sum(jnp.transpose(lanes), axis=0, keepdims=True)
    out[...] = term_in + term_out


def retain_product(where, *refs):
    blocks, (w_out, mine, theirs, acc) = refs[:8], refs[8:]
    t = pl.program_id(0)
    act = jnp.concatenate([b[...] for b in blocks], axis=0)
    part = jnp.dot(act, w_out[...], preferred_element_type=F32)

    @pl.when(t == 0)
    def _():
        acc[...] = part

    @pl.when(t > 0)
    def _():
        acc[...] += part

    @pl.when(t == pl.num_programs(0) - 1)
    def _():
        mine[...] = acc[0:128, :]
        for j in range(4):
            for i in range(4):
                at = 128 + (j * 4 + i) * 8
                theirs[(i * 4 + j) * 8 : (i * 4 + j) * 8 + 8, :] = acc[at : at + 8, :]


def call(kernel, where, args, outs, scratch=(), steps=6):
    def spec(shape, block, index):
        if block is None:
            return pl.BlockSpec(shape, lambda t, w: (0,) * len(shape))
        return pl.BlockSpec(block, index)

    return pl.pallas_call(
        kernel,
        grid_spec=pltpu.PrefetchScalarGridSpec(
            num_scalar_prefetch=1,
            grid=(steps,),
            in_specs=[spec(a.shape, b, i) for a, b, i in args],
            out_specs=[spec(s, b, i) for s, _, b, i in outs],
            scratch_shapes=list(scratch),
        ),
        out_shape=[jax.ShapeDtypeStruct(s, d) for s, d, _, _ in outs],
        compiler_params=pltpu.CompilerParams(vmem_limit_bytes=40 * 2**20),
        cost_estimate=pl.CostEstimate(flops=1, bytes_accessed=1, transcendentals=0),
    )(where, *[a for a, _, _ in args])


def whole(a):
    return (a, None, None)


def by_n(a, tile=TILE):
    return (a, (a.shape[0], tile), lambda t, w: (0, t))


def out_n(rows, n, dtype, tile=TILE):
    return ((rows, n), dtype, (rows, tile), lambda t, w: (0, t))


def drop_where(kernel):
    def inner(where, *refs):
        kernel(*refs)

    return inner


def permutes(parts, shift, sign=1):
    return [lax.ppermute(parts[k], "col", shift(sign * (k + 1))) for k in range(3)]


def after(value, *others):
    return lax.optimization_barrier((value, *others))[0]


def local(
    forget_tokens,
    forget_cotangent,
    forget_labels,
    retain_tokens,
    ln_gain,
    w_in,
    b_in,
    w_out,
    b_out,
    pruned,
):
    core = lax.axis_index("dp")
    row = lax.axis_index("row")
    col = lax.axis_index("col")
    y, z = col % 4, col // 4
    width = w_in.shape[0]
    half = w_in.shape[1] // 2
    steps = half // TILE
    where = jnp.stack([core, y, z]).astype(jnp.int32)
    gain = ln_gain[None, :]

    own = (forget_tokens, forget_cotangent * forget_labels[:, None].astype(BF16), retain_tokens)
    other = lax.ppermute(jnp.concatenate(own, axis=0), "dp", SWAP)

    def third(k):
        return (other, (128, width), lambda t, w: (k, 0))

    w_in_tile = (w_in, (width, TILE), lambda t, w: (0, w[0] * steps + t))
    w_out_tile = (w_out, (TILE, width), lambda t, w: (w[0] * steps + t, 0))
    parts_out = [out_n(96, half, BF16)] * 4 + [((128, width), BF16, None, None)]
    lhs = pltpu.VMEM((256, width), BF16)
    weights = [whole(gain), w_in_tile, w_out_tile]
    a_parts = call(
        functools.partial(partials, False),
        where,
        [whole(v) for v in own] + weights,
        parts_out,
        [lhs],
        steps,
    )
    a_got = permutes(a_parts[1:4], shift_y)
    b_parts = call(
        functools.partial(partials, True),
        where,
        [third(0), third(1), third(2)] + weights,
        parts_out + [out_n(8, half, F32)],
        [pltpu.VMEM((48, width), BF16), lhs],
        steps,
    )
    b_got = permutes(b_parts[1:4], shift_z)
    g_own, g_other, g_part = a_parts[4], b_parts[4], b_parts[5]

    other_s, _ = lax.optimization_barrier((other, b_parts[0]))
    tokens = jnp.stack(
        [forget_tokens, retain_tokens, other_s[:128], other_s[256:]]
    ).astype(F32)
    part_mean = jnp.sum(tokens, axis=2) / width
    centred = tokens - part_mean[..., None]
    part_m2 = jnp.sum(centred * centred, axis=2)
    share = jnp.concatenate([part_mean, part_m2, g_part[0].reshape(half // 128, 128)])
    share, _ = lax.optimization_barrier((share, a_got[0]))
    share = lax.all_to_all(
        jnp.broadcast_to(share[None], (16,) + share.shape), "col", 0, 0, tiled=True
    )
    g_all = share[:, 8:].reshape(16, half)
    stats = share[:, 0:8].transpose(1, 2, 0)
    owned = lax.dynamic_slice_in_dim(stats, (y * 4 + z) * 8, 8, 1)

    def of_set(k):
        return (owned[2 * k : 2 * k + 2].reshape(16, 16), owned[4 + 2 * k : 6 + 2 * k].reshape(16, 16))

    normed_t = call(
        functools.partial(normalise, width),
        where,
        [whole(forget_tokens), third(0), whole(stats[0:4:2].reshape(256, 16)),
         whole(stats[4:8:2].reshape(256, 16)), whole(gain)],
        [((width, 256), BF16, None, None)],
        (),
        1,
    )[0]

    b_half = lax.dynamic_slice_in_dim(b_in, core * half, half, 0)[None, :]
    ids = row * w_in.shape[1] + core * half + jnp.arange(half, dtype=jnp.int32)
    is_pruned = jnp.any(pruned[:, None] == ids[None, :], axis=0)
    keep = jnp.where(is_pruned, 0.0, 1.0)[None, :]

    def join(*lists):
        flat = lax.optimization_barrier(tuple(v for group in lists for v in group))
        at, out = 0, []
        for group in lists:
            out.append(list(flat[at : at + len(group)]))
            at += len(group)
        return out

    def wide(kernel, args, extra, outs):
        return call(
            drop_where(kernel),
            where,
            [by_n(v, WIDE) for v in args] + extra,
            [out_n(rows, half, kind, WIDE) for rows, kind in outs],
            steps=half // WIDE,
        )

    def sums_of(parts, got):
        return wide(stage_sum, [parts[0]] + got, [], [(24, F32)] + [(24, BF16)] * 3)

    def block_of(k, sums, back):
        extra = [whole(v) for v in of_set(k)] + [by_n(v, WIDE) for v in (g_all, b_half, keep)]
        kernel = functools.partial(activate, width)
        return wide(kernel, [sums[0]] + back, extra, [(24, BF16)])[0]

    def regrouped(block, near):
        return wide(regroup, [block] + near, [], [(64, BF16), (32, BF16)])

    a_got, b_got = join(a_got, b_got)
    a_sums, b_sums = sums_of(a_parts, a_got), sums_of(b_parts, b_got)
    a_back, b_back = join(permutes(a_sums[1:], shift_z), permutes(b_sums[1:], shift_y))
    a_block, b_block = block_of(0, a_sums, a_back), block_of(1, b_sums, b_back)
    a_near, b_near = join(
        permutes([a_block] * 3, shift_z, -1), permutes([b_block] * 3, shift_y, -1)
    )
    a_forget, a_retain = regrouped(a_block, a_near)
    b_forget, b_retain = regrouped(b_block, b_near)
    a_far, b_far = permutes([a_forget] * 3, shift_y, -1), permutes([b_forget] * 3, shift_z, -1)
    a_forget, b_forget = [a_forget] + a_far, [b_forget] + b_far
    a_retain, b_retain, _ = lax.optimization_barrier((a_retain, b_retain, a_far[0]))
    a_retain = [a_retain] + permutes([a_retain] * 3, shift_y, -1)
    b_retain = [b_retain] + permutes([b_retain] * 3, shift_z, -1)

    terms = call(
        saliency_terms,
        where,
        [by_n(v) for v in a_forget + b_forget]
        + [whole(normed_t), whole(g_own), whole(g_other), w_in_tile, w_out_tile],
        [out_n(1, half, F32)],
        (),
        steps,
    )[0]
    terms = jnp.broadcast_to(terms.reshape(1, half // 128, 128), (32, half // 128, 128))
    terms = lax.all_to_all(terms, ("dp", "col"), 0, 0, tiled=True)
    saliency = jnp.sum(terms.reshape(2, 16, half), axis=1).reshape(2 * half) / D

    mine, theirs = call(
        retain_product,
        where,
        [by_n(v) for v in a_retain + b_retain] + [w_out_tile],
        [((128, width), F32, None, None)] * 2,
        [pltpu.VMEM((256, width), F32)],
        steps,
    )
    mine = (mine + lax.ppermute(theirs, "dp", SWAP)).reshape(4, 4, 8, width)

    def for_row(r):
        return lax.dynamic_index_in_dim(mine, (r - y) % 4, 0, keepdims=False)

    total = for_row(row)
    for k in (1, 2, 3):
        total = total + lax.ppermute(for_row(row + k), "row", shift_row(k))
    retain_out = (total + b_out).astype(BF16)
    retain_out = lax.dynamic_slice_in_dim(
        jnp.concatenate([retain_out, retain_out], axis=0), (4 - z) % 4, 4, 0
    ).reshape(32, width)
    return (saliency, retain_out)


def solution(mesh):
    in_specs = (
        P("dp", "col"),
        P("dp", "col"),
        P("dp"),
        P("dp", "col"),
        P("col"),
        P("col", "row"),
        P("row"),
        P("row", "col"),
        P("col"),
        P("row"),
    )
    out_specs = (P("row"), P(("dp", "row"), "col"))
    return jax.shard_map(local, mesh=mesh, in_specs=in_specs, out_specs=out_specs, check_vma=False)
```

```python
import functools

import jax
import jax.numpy as jnp
from jax import lax
from jax.experimental import pallas as pl
from jax.experimental.pallas import tpu as pltpu
from jax.sharding import PartitionSpec as P

D = 6144
BF16 = jnp.bfloat16
F32 = jnp.float32
TILE = 512
WIDE = 1024
SMALL = 16 * 2**20


def gelu_exact(v):
    return v * 0.5 * (1.0 + lax.erf(v * 0.7071067811865476))


def gelu_slope(v):
    return (
        0.5 * (1.0 + lax.erf(v * 0.7071067811865476))
        + v * jnp.exp(-0.5 * v * v) * 0.3989422804014327
    )


def pairs(first, k):
    out = []
    for core in range(2):
        for z in range(4):
            for y in range(4):
                if (core == 0) == first:
                    to = z * 4 + (y + k) % 4
                else:
                    to = ((z + k) % 4) * 4 + y
                out.append((core * 16 + z * 4 + y, core * 16 + to))
    return out


def shift_row(k):
    return [(r, (r + k) % 4) for r in range(4)]


SWAP = [(0, 1), (1, 0)]


def row_order(where):
    p = lax.broadcasted_iota(jnp.int32, (256, 256), 0)
    q = lax.broadcasted_iota(jnp.int32, (256, 256), 1)
    e, h, i, j = p & 7, (p >> 3) & 1, (p >> 4) & 3, p >> 6
    second = where[0] == 1
    by = (where[1] + jnp.where(second, i, j)) & 3
    bz = (where[2] + jnp.where(second, j, i)) & 3
    return jnp.where(h * 128 + (by * 4 + bz) * 8 + e == q, 1.0, 0.0).astype(BF16)


def reorder(sel, x):
    return jnp.dot(sel, x, preferred_element_type=F32).astype(BF16)


def grad_partials(where, own, other, w_out, o0, o1, o2, o3, rows):
    @pl.when(pl.program_id(0) == 0)
    def _():
        rows[...] = reorder(row_order(where), jnp.concatenate([own[...], other[...]], axis=0))

    grad = lax.dot_general(
        rows[...], w_out[...], (((1,), (1,)), ((), ())), preferred_element_type=F32
    ).astype(BF16)
    for j, o in enumerate((o0, o1, o2, o3)):
        o[...] = grad[j * 64 : j * 64 + 64]


def merged_stats(width, stats, core):
    part = stats[pl.ds(core * 16, 16)]
    means, m2 = part[:, 0:2], part[:, 2:4]
    mean = jnp.sum(means, axis=0) / 16
    gap = means - mean[None]
    var = (jnp.sum(m2, axis=0) + width * jnp.sum(gap * gap, axis=0)) / D
    rows = jnp.concatenate([mean, lax.rsqrt(var + 1e-06), mean, mean], axis=0)
    return jnp.transpose(rows)


def normed_rows(x, merged, k, gain):
    x = (x[...].astype(F32) - merged[:, k : k + 1]) * merged[:, 2 + k : 3 + k] * gain[...]
    return x.astype(BF16)


def pre_partials(
    width, where, own_f, own_r, other_f, other_r, stats, gain, w_in, o0, o1, o2, o3, normed_t, lhs
):
    @pl.when(pl.program_id(0) == 0)
    def _():
        own = merged_stats(width, stats, where[0])
        other = merged_stats(width, stats, 1 - where[0])
        x_f = [normed_rows(own_f, own, 0, gain), normed_rows(other_f, other, 0, gain)]
        x_r = [normed_rows(own_r, own, 1, gain), normed_rows(other_r, other, 1, gain)]
        sel = row_order(where)
        rows = jnp.dot(sel, jnp.concatenate(x_f, axis=0), preferred_element_type=F32)
        lhs[0:256, :] = rows.astype(BF16)
        normed_t[...] = jnp.transpose(rows).astype(BF16)
        lhs[256:512, :] = reorder(sel, jnp.concatenate(x_r, axis=0))

    pre = jnp.dot(lhs[...], w_in[...], preferred_element_type=F32).astype(BF16)
    for j, o in enumerate((o0, o1, o2, o3)):
        for i in range(4):
            at = (j * 4 + i) * 16
            o[i * 32 : i * 32 + 16, :] = pre[at : at + 16]
            o[i * 32 + 16 : i * 32 + 32, :] = pre[256 + at : 256 + at + 16]


def stage_sum(p0, p1, p2, p3, g0, g1, g2, g3, keep, *sends):
    for i in range(4):
        parts = []
        for rows, (a, b, c, d) in ((32, (p0, p1, p2, p3)), (16, (g0, g1, g2, g3))):
            at = slice(i * rows, (i + 1) * rows)
            parts.append(
                (a[at, :].astype(F32) + b[at, :].astype(F32))
                + (c[at, :].astype(F32) + d[at, :].astype(F32))
            )
        total = jnp.concatenate(parts, axis=0)
        if i == 0:
            keep[...] = total
        else:
            sends[i - 1][...] = total.astype(BF16)


def activate(keep, a, b, c, bias, mask, out):
    total = (keep[...] + a[...].astype(F32)) + (b[...].astype(F32) + c[...].astype(F32))
    pre = total[:32] + bias[...]
    act = gelu_exact(pre)
    out[0:16, :] = act[:16].astype(BF16)
    out[16:32, :] = (total[32:48] * gelu_slope(pre[:16])).astype(BF16)
    out[32:48, :] = (act[16:32].astype(BF16).astype(F32) * mask[...]).astype(BF16)


def regroup(b0, b1, b2, b3, forget, retain):
    for i, b in enumerate((b0, b1, b2, b3)):
        at = i * 16
        forget[at : at + 16, :] = b[0:16, :]
        forget[64 + at : 64 + at + 16, :] = b[16:32, :]
        retain[at : at + 16, :] = b[32:48, :]


def saliency_terms(where, b0, b1, b2, b3, normed_t, grad_y, w_in, w_out, out):
    blocks = (b0, b1, b2, b3)
    act = jnp.concatenate([b[0:64, :] for b in blocks], axis=0)
    grad_pre = jnp.concatenate([b[64:128, :] for b in blocks], axis=0)
    grad_in = jnp.dot(normed_t[...], grad_pre, preferred_element_type=F32)
    grad_out = lax.dot_general(
        act, grad_y[...], (((0,), (0,)), ((), ())), preferred_element_type=F32
    )
    term_in = jnp.sum(jnp.abs(w_in[...].astype(F32) * grad_in), axis=0, keepdims=True)
    prod = jnp.abs(w_out[...].astype(F32) * grad_out)
    lanes = (prod[:, 0:128] + prod[:, 128:256]) + prod[:, 256:384]
    term_out = jnp.sum(jnp.transpose(lanes), axis=0, keepdims=True)
    out[...] = term_in + term_out


def retain_product(where, b0, b1, b2, b3, w_out, mine, theirs, acc):
    t = pl.program_id(0)
    act = jnp.concatenate([b0[...], b1[...], b2[...], b3[...]], axis=0)
    part = jnp.dot(act, w_out[...], preferred_element_type=F32)

    @pl.when(t == 0)
    def _():
        acc[...] = part

    @pl.when(t > 0)
    def _():
        acc[...] += part

    def store(swap):
        for j in range(4):
            for i in range(4):
                at = (j * 4 + i) * 16
                to = (i * 4 + j if swap else j * 4 + i) * 8
                mine[to : to + 8, :] = acc[at : at + 8, :]
                theirs[to : to + 8, :] = acc[at + 8 : at + 16, :]

    last = t == pl.num_programs(0) - 1

    @pl.when(last & (where[0] == 0))
    def _():
        store(False)

    @pl.when(last & (where[0] == 1))
    def _():
        store(True)


def call(kernel, where, args, outs, scratch=(), steps=6, vmem=None):
    def spec(shape, block, index):
        if block is None:
            return pl.BlockSpec(shape, lambda t, w: (0,) * len(shape))
        return pl.BlockSpec(block, index)

    return pl.pallas_call(
        kernel,
        grid_spec=pltpu.PrefetchScalarGridSpec(
            num_scalar_prefetch=1,
            grid=(steps,),
            in_specs=[spec(a.shape, b, i) for a, b, i in args],
            out_specs=[spec(s, b, i) for s, _, b, i in outs],
            scratch_shapes=list(scratch),
        ),
        out_shape=[jax.ShapeDtypeStruct(s, d) for s, d, _, _ in outs],
        compiler_params=pltpu.CompilerParams(vmem_limit_bytes=vmem),
        cost_estimate=pl.CostEstimate(flops=1, bytes_accessed=1, transcendentals=0),
    )(where, *[a for a, _, _ in args])


def whole(a):
    return (a, None, None)


def by_n(a, tile=TILE):
    return (a, (a.shape[0], tile), lambda t, w: (0, t))


def out_n(rows, n, dtype, tile=TILE):
    return ((rows, n), dtype, (rows, tile), lambda t, w: (0, t))


def drop_where(kernel):
    def inner(where, *refs):
        kernel(*refs)

    return inner


def permutes(parts, first, sign=1):
    return [
        lax.ppermute(parts[k], ("dp", "col"), pairs(first, sign * (k + 1))) for k in range(3)
    ]


def local(
    forget_tokens,
    forget_cotangent,
    forget_labels,
    retain_tokens,
    ln_gain,
    w_in,
    b_in,
    w_out,
    b_out,
    pruned,
):
    core = lax.axis_index("dp")
    row = lax.axis_index("row")
    col = lax.axis_index("col")
    y, z = col % 4, col // 4
    width = w_in.shape[0]
    half = w_in.shape[1] // 2
    steps = half // TILE
    where = jnp.stack([core, y, z]).astype(jnp.int32)
    gain = ln_gain[None, :]

    tokens = jnp.stack([forget_tokens, retain_tokens]).astype(F32)
    part_mean = jnp.sum(tokens, axis=2) / width
    centred = tokens - part_mean[..., None]
    part_m2 = jnp.sum(centred * centred, axis=2)
    stats = jnp.broadcast_to(jnp.concatenate([part_mean, part_m2])[None], (32, 4, 128))
    stats = lax.all_to_all(stats, ("dp", "col"), 0, 0, tiled=True)

    own_g = forget_cotangent * forget_labels[:, None].astype(BF16)
    other = lax.ppermute(
        jnp.concatenate([forget_tokens, own_g, retain_tokens], axis=0), "dp", SWAP
    )

    def third(k):
        return (other, (128, width), lambda t, w: (k, 0))

    w_in_tile = (w_in, (width, TILE), lambda t, w: (0, w[0] * steps + t))
    w_out_tile = (w_out, (TILE, width), lambda t, w: (w[0] * steps + t, 0))
    *g_parts, grad_y = call(
        grad_partials,
        where,
        [whole(own_g), third(1), w_out_tile],
        [out_n(64, half, BF16)] * 4 + [((256, width), BF16, None, None)],
        (),
        steps,
    )
    g_got = permutes(g_parts[1:], True)
    stats, _ = lax.optimization_barrier((stats, g_parts[0]))
    *p_parts, normed_t = call(
        functools.partial(pre_partials, width),
        where,
        [whole(forget_tokens), whole(retain_tokens), third(0), third(2), whole(stats),
         whole(gain), w_in_tile],
        [out_n(128, half, BF16)] * 4 + [((width, 256), BF16, None, None)],
        [pltpu.VMEM((512, width), BF16)],
        steps,
    )
    p_got = permutes(p_parts[1:], True)

    b_half = lax.dynamic_slice_in_dim(b_in, core * half, half, 0)[None, :]
    ids = row * w_in.shape[1] + core * half + jnp.arange(half, dtype=jnp.int32)
    is_pruned = jnp.any(pruned[:, None] == ids[None, :], axis=0)
    keep = jnp.where(is_pruned, 0.0, 1.0)[None, :]

    def wide(kernel, args, outs):
        return call(
            drop_where(kernel),
            where,
            [by_n(v, WIDE) for v in args],
            [out_n(rows, half, kind, WIDE) for rows, kind in outs],
            steps=half // WIDE,
            vmem=SMALL,
        )

    sums = wide(
        stage_sum,
        [p_parts[0]] + p_got + [g_parts[0]] + g_got,
        [(48, F32)] + [(48, BF16)] * 3,
    )
    back = permutes(sums[1:], False)
    block = wide(activate, [sums[0]] + back + [b_half, keep], [(48, BF16)])[0]
    near = permutes([block] * 3, False, -1)
    forget, retain = wide(regroup, [block] + near, [(128, BF16), (64, BF16)])
    far = permutes([forget] * 3, True, -1)
    retain, _ = lax.optimization_barrier((retain, far[0]))
    retain_far = permutes([retain] * 3, True, -1)

    terms = call(
        saliency_terms,
        where,
        [by_n(v) for v in [forget] + far] + [whole(normed_t), whole(grad_y), w_in_tile, w_out_tile],
        [out_n(1, half, F32)],
        (),
        steps,
    )[0]
    terms = jnp.broadcast_to(terms.reshape(1, half // 128, 128), (32, half // 128, 128))
    terms = lax.all_to_all(terms, ("dp", "col"), 0, 0, tiled=True)
    saliency = jnp.sum(terms.reshape(2, 16, half), axis=1).reshape(2 * half) / D

    mine, theirs = call(
        retain_product,
        where,
        [by_n(v) for v in [retain] + retain_far] + [w_out_tile],
        [((128, width), F32, None, None)] * 2,
        [pltpu.VMEM((256, width), F32)],
        steps,
    )
    mine = (mine + lax.ppermute(theirs, "dp", SWAP)).reshape(4, 4, 8, width)

    def for_row(r):
        return lax.dynamic_index_in_dim(mine, (r - y) % 4, 0, keepdims=False)

    total = for_row(row)
    for k in (1, 2, 3):
        total = total + lax.ppermute(for_row(row + k), "row", shift_row(k))
    retain_out = (total + b_out).astype(BF16)
    retain_out = lax.dynamic_slice_in_dim(
        jnp.concatenate([retain_out, retain_out], axis=0), (4 - z) % 4, 4, 0
    ).reshape(32, width)
    return (saliency, retain_out)


def solution(mesh):
    in_specs = (
        P("dp", "col"),
        P("dp", "col"),
        P("dp"),
        P("dp", "col"),
        P("col"),
        P("col", "row"),
        P("row"),
        P("row", "col"),
        P("col"),
        P("row"),
    )
    out_specs = (P("row"), P(("dp", "row"), "col"))
    return jax.shard_map(local, mesh=mesh, in_specs=in_specs, out_specs=out_specs, check_vma=False)
```

```python
import functools

import jax
import jax.numpy as jnp
from jax import lax
from jax.experimental import pallas as pl
from jax.experimental.pallas import tpu as pltpu
from jax.sharding import PartitionSpec as P

D = 6144
BF16 = jnp.bfloat16
F32 = jnp.float32
TILE = 1536
WIDE = 1536
SMALL = 16 * 2**20


def gelu_exact(v):
    return v * 0.5 * (1.0 + lax.erf(v * 0.7071067811865476))


def gelu_slope(v):
    return (
        0.5 * (1.0 + lax.erf(v * 0.7071067811865476))
        + v * jnp.exp(-0.5 * v * v) * 0.3989422804014327
    )


def pairs(first, k):
    out = []
    for core in range(2):
        for z in range(4):
            for y in range(4):
                if (core == 0) == first:
                    to = z * 4 + (y + k) % 4
                else:
                    to = ((z + k) % 4) * 4 + y
                out.append((core * 16 + z * 4 + y, core * 16 + to))
    return out


def shift_row(k):
    return [(r, (r + k) % 4) for r in range(4)]


SWAP = [(0, 1), (1, 0)]


def row_order(where):
    p = lax.broadcasted_iota(jnp.int32, (256, 256), 0)
    q = lax.broadcasted_iota(jnp.int32, (256, 256), 1)
    e, h, i, j = p & 7, (p >> 3) & 1, (p >> 4) & 3, p >> 6
    second = where[0] == 1
    by = (where[1] + jnp.where(second, i, j)) & 3
    bz = (where[2] + jnp.where(second, j, i)) & 3
    return jnp.where(h * 128 + (by * 4 + bz) * 8 + e == q, 1.0, 0.0).astype(BF16)


def reorder(sel, x):
    return jnp.dot(sel, x, preferred_element_type=F32).astype(BF16)


def partials(where, f0, f1, g0, g1, r0, r1, gain, w_in, w_out, *rest):
    outs, (rows_g, g_out, lhs, lhs_gain) = rest[:4], rest[4:]

    @pl.when(pl.program_id(0) == 0)
    def _():
        sel = row_order(where)

        def centred(own, other):
            x = jnp.concatenate([own[...], other[...]], axis=0).astype(F32)
            mean = jnp.sum(x, axis=1, keepdims=True) / x.shape[1]
            return ((x - mean) * gain[...]).astype(BF16)

        lhs[0:256, :] = reorder(sel, centred(f0, f1))
        lhs[256:512, :] = reorder(sel, centred(r0, r1))
        rows_g[...] = reorder(sel, jnp.concatenate([g0[...], g1[...]], axis=0))
        a = jnp.broadcast_to(gain[...], (16, gain.shape[1]))
        for k in range(3):
            part = a.astype(BF16)
            lhs_gain[k * 16 : k * 16 + 16, :] = part
            a = a - part.astype(F32)

    pre = jnp.dot(lhs[...], w_in[...], preferred_element_type=F32).astype(BF16)
    grad = lax.dot_general(
        rows_g[...], w_out[...], (((1,), (1,)), ((), ())), preferred_element_type=F32
    ).astype(BF16)
    for j, o in enumerate(outs):
        for i in range(4):
            at, to = (j * 4 + i) * 16, i * 48
            o[to : to + 16, :] = pre[at : at + 16]
            o[to + 16 : to + 32, :] = pre[256 + at : 256 + at + 16]
            o[to + 32 : to + 48, :] = grad[at : at + 16]
    g = jnp.dot(lhs_gain[...], w_in[...], preferred_element_type=F32)
    g_out[...] = (g[32:40] + g[16:24]) + g[0:8]


def stage_sum(own, a, b, c, keep, *sends):
    for i in range(4):
        at = slice(i * 48, i * 48 + 48)
        total = (own[at, :].astype(F32) + a[at, :].astype(F32)) + (
            b[at, :].astype(F32) + c[at, :].astype(F32)
        )
        if i == 0:
            keep[...] = total
        else:
            sends[i - 1][...] = total.astype(BF16)


def merged(width, means, m2):
    gap = means - jnp.sum(means, axis=1, keepdims=True) / 16
    var = (
        jnp.sum(m2, axis=1, keepdims=True) + width * jnp.sum(gap * gap, axis=1, keepdims=True)
    ) / D
    return gap, lax.rsqrt(var + 1e-06)


def activate(width, keep, a, b, c, means, m2, g_all, bias, mask, out):
    total = (keep[...] + a[...].astype(F32)) + (b[...].astype(F32) + c[...].astype(F32))
    gap, scale = merged(width, means[...], m2[...])
    pre = total[:32]
    for s in range(16):
        pre = pre + gap[:, s : s + 1] * g_all[s : s + 1, :]
    pre = scale * pre + bias[...]
    act = gelu_exact(pre)
    out[0:16, :] = act[:16].astype(BF16)
    out[16:32, :] = (total[32:48] * gelu_slope(pre[:16])).astype(BF16)
    out[32:48, :] = (act[16:32].astype(BF16).astype(F32) * mask[...]).astype(BF16)


def normalise(width, where, own, other, means, m2, gain, out):
    x = jnp.concatenate([own[...], other[...]], axis=0).astype(F32)
    m = means[...]
    _, scale = merged(width, m, m2[...])
    mean = jnp.sum(m, axis=1, keepdims=True) / 16
    x = ((x - mean) * scale * gain[...]).astype(BF16)
    rows = jnp.dot(row_order(where), x, preferred_element_type=F32)
    out[...] = jnp.transpose(rows).astype(BF16)


def regroup(b0, b1, b2, b3, forget, retain):
    for i, b in enumerate((b0, b1, b2, b3)):
        at = i * 16
        forget[at : at + 16, :] = b[0:16, :]
        forget[64 + at : 64 + at + 16, :] = b[16:32, :]
        retain[at : at + 16, :] = b[32:48, :]


def saliency_terms(where, b0, b1, b2, b3, normed_t, grad_y, w_in, w_out, out):
    blocks = (b0, b1, b2, b3)
    act = jnp.concatenate([b[0:64, :] for b in blocks], axis=0)
    grad_pre = jnp.concatenate([b[64:128, :] for b in blocks], axis=0)
    grad_in = jnp.dot(normed_t[...], grad_pre, preferred_element_type=F32)
    grad_out = lax.dot_general(
        act, grad_y[...], (((0,), (0,)), ((), ())), preferred_element_type=F32
    )
    term_in = jnp.sum(jnp.abs(w_in[...].astype(F32) * grad_in), axis=0, keepdims=True)
    prod = jnp.abs(w_out[...].astype(F32) * grad_out)
    lanes = (prod[:, 0:128] + prod[:, 128:256]) + prod[:, 256:384]
    term_out = jnp.sum(jnp.transpose(lanes), axis=0, keepdims=True)
    out[...] = jnp.broadcast_to((term_in + term_out)[None], out.shape)


def retain_product(where, b0, b1, b2, b3, w_out, mine, theirs, acc):
    t = pl.program_id(0)
    act = jnp.concatenate([b0[...], b1[...], b2[...], b3[...]], axis=0)
    part = jnp.dot(act, w_out[...], preferred_element_type=F32)

    @pl.when(t == 0)
    def _():
        acc[...] = part

    @pl.when(t > 0)
    def _():
        acc[...] += part

    def store(swap):
        for j in range(4):
            for i in range(4):
                at = (j * 4 + i) * 16
                to = (i * 4 + j if swap else j * 4 + i) * 8
                mine[to : to + 8, :] = acc[at : at + 8, :]
                theirs[to : to + 8, :] = acc[at + 8 : at + 16, :]

    last = t == pl.num_programs(0) - 1

    @pl.when(last & (where[0] == 0))
    def _():
        store(False)

    @pl.when(last & (where[0] == 1))
    def _():
        store(True)


def call(kernel, where, args, outs, scratch=(), steps=6, vmem=None):
    def spec(shape, block, index):
        if block is None:
            return pl.BlockSpec(shape, lambda t, w: (0,) * len(shape))
        return pl.BlockSpec(block, index)

    return pl.pallas_call(
        kernel,
        grid_spec=pltpu.PrefetchScalarGridSpec(
            num_scalar_prefetch=1,
            grid=(steps,),
            in_specs=[spec(a.shape, b, i) for a, b, i in args],
            out_specs=[spec(s, b, i) for s, _, b, i in outs],
            scratch_shapes=list(scratch),
        ),
        out_shape=[jax.ShapeDtypeStruct(s, d) for s, d, _, _ in outs],
        compiler_params=pltpu.CompilerParams(vmem_limit_bytes=vmem),
        cost_estimate=pl.CostEstimate(flops=1, bytes_accessed=1, transcendentals=0),
    )(where, *[a for a, _, _ in args])


def whole(a):
    return (a, None, None)


def by_n(a, tile=TILE):
    return (a, (a.shape[0], tile), lambda t, w: (0, t))


def out_n(rows, n, dtype, tile=TILE):
    return ((rows, n), dtype, (rows, tile), lambda t, w: (0, t))


def drop_where(kernel):
    def inner(where, *refs):
        kernel(*refs)

    return inner


def permutes(parts, first, sign=1):
    return [
        lax.ppermute(parts[k], ("dp", "col"), pairs(first, sign * (k + 1))) for k in range(3)
    ]


def local(
    forget_tokens,
    forget_cotangent,
    forget_labels,
    retain_tokens,
    ln_gain,
    w_in,
    b_in,
    w_out,
    b_out,
    pruned,
):
    core = lax.axis_index("dp")
    row = lax.axis_index("row")
    col = lax.axis_index("col")
    y, z = col % 4, col // 4
    width = w_in.shape[0]
    half = w_in.shape[1] // 2
    steps = half // TILE
    where = jnp.stack([core, y, z]).astype(jnp.int32)
    gain = ln_gain[None, :]

    own_g = forget_cotangent * forget_labels[:, None].astype(BF16)
    other = lax.ppermute(
        jnp.concatenate([forget_tokens, own_g, retain_tokens], axis=0), "dp", SWAP
    )

    def third(k):
        return (other, (128, width), lambda t, w: (k, 0))

    w_in_tile = (w_in, (width, TILE), lambda t, w: (0, w[0] * steps + t))
    w_out_tile = (w_out, (TILE, width), lambda t, w: (w[0] * steps + t, 0))
    *parts, grad_y, g_part = call(
        partials,
        where,
        [whole(forget_tokens), third(0), whole(own_g), third(1), whole(retain_tokens), third(2),
         whole(gain), w_in_tile, w_out_tile],
        [out_n(192, half, BF16)] * 4 + [((256, width), BF16, None, None), out_n(8, half, F32)],
        [pltpu.VMEM((512, width), BF16), pltpu.VMEM((48, width), BF16)],
        steps,
    )
    got = permutes(parts[1:], True)

    tokens = jnp.stack([forget_tokens, retain_tokens, other[:128], other[256:]])
    tokens, _ = lax.optimization_barrier((tokens, parts[0]))
    tokens = tokens.astype(F32)
    part_mean = jnp.sum(tokens, axis=2) / width
    centred = tokens - part_mean[..., None]
    part_m2 = jnp.sum(centred * centred, axis=2)
    share = jnp.concatenate([part_mean, part_m2, g_part[0].reshape(half // 128, 128)])
    share = jnp.broadcast_to(share[None], (16,) + share.shape)
    share = lax.all_to_all(share, "col", 0, 0, tiled=True)
    g_all = share[:, 8:].reshape(16, half)
    stats = share[:, 0:8].transpose(1, 2, 0)
    owned = lax.dynamic_slice_in_dim(stats, (y * 4 + z) * 8, 8, 1)
    owned = owned.reshape(2, 2, 2, 8, 16).transpose(0, 2, 1, 3, 4).reshape(2, 32, 16)
    normed_t = call(
        functools.partial(normalise, width),
        where,
        [whole(forget_tokens), third(0), whole(stats[0:4:2].reshape(256, 16)),
         whole(stats[4:8:2].reshape(256, 16)), whole(gain)],
        [((width, 256), BF16, None, None)],
        (),
        1,
    )[0]

    b_half = lax.dynamic_slice_in_dim(b_in, core * half, half, 0)[None, :]
    ids = row * w_in.shape[1] + core * half + jnp.arange(half, dtype=jnp.int32)
    is_pruned = jnp.any(pruned[:, None] == ids[None, :], axis=0)
    keep = jnp.where(is_pruned, 0.0, 1.0)[None, :]

    def wide(kernel, args, outs, extra=()):
        return call(
            drop_where(kernel),
            where,
            [by_n(v, WIDE) for v in args] + [whole(v) for v in extra],
            [out_n(rows, half, kind, WIDE) for rows, kind in outs],
            steps=half // WIDE,
            vmem=SMALL,
        )

    sums = wide(stage_sum, [parts[0]] + got, [(48, F32)] + [(48, BF16)] * 3)
    back = permutes(sums[1:], False)

    def act(keep, a, b, c, g_all, bias, mask, means, m2, out):
        activate(width, keep, a, b, c, means, m2, g_all, bias, mask, out)

    block = wide(act, [sums[0]] + back + [g_all, b_half, keep], [(48, BF16)], (owned[0], owned[1]))[0]
    near = permutes([block] * 3, False, -1)
    forget, retain = wide(regroup, [block] + near, [(128, BF16), (64, BF16)])
    far = permutes([forget] * 3, True, -1)
    retain, _ = lax.optimization_barrier((retain, far[0]))
    retain_far = permutes([retain] * 3, True, -1)

    terms = call(
        saliency_terms,
        where,
        [by_n(v) for v in [forget] + far] + [whole(normed_t), whole(grad_y), w_in_tile, w_out_tile],
        [((32, 1, half), F32, (32, 1, TILE), lambda t, w: (0, 0, t))],
        (),
        steps,
    )[0]
    terms = lax.all_to_all(terms, ("dp", "col"), 0, 0, tiled=True)
    saliency = jnp.sum(terms.reshape(2, 16, half), axis=1).reshape(2 * half) / D

    mine, theirs = call(
        retain_product,
        where,
        [by_n(v) for v in [retain] + retain_far] + [w_out_tile],
        [((128, width), F32, None, None)] * 2,
        [pltpu.VMEM((256, width), F32)],
        steps,
    )
    mine = (mine + lax.ppermute(theirs, "dp", SWAP)).reshape(4, 4, 8, width)

    def for_row(r):
        return lax.dynamic_index_in_dim(mine, (r - y) % 4, 0, keepdims=False)

    total = for_row(row)
    for k in (1, 2, 3):
        total = total + lax.ppermute(for_row(row + k), "row", shift_row(k))
    retain_out = (total + b_out).astype(BF16)
    retain_out = lax.dynamic_slice_in_dim(
        jnp.concatenate([retain_out, retain_out], axis=0), (4 - z) % 4, 4, 0
    ).reshape(32, width)
    return (saliency, retain_out)


def solution(mesh):
    in_specs = (
        P("dp", "col"),
        P("dp", "col"),
        P("dp"),
        P("dp", "col"),
        P("col"),
        P("col", "row"),
        P("row"),
        P("row", "col"),
        P("col"),
        P("row"),
    )
    out_specs = (P("row"), P(("dp", "row"), "col"))
    return jax.shard_map(local, mesh=mesh, in_specs=in_specs, out_specs=out_specs, check_vma=False)
```

```python
import functools

import jax
import jax.numpy as jnp
from jax import lax
from jax.experimental import pallas as pl
from jax.experimental.pallas import tpu as pltpu
from jax.sharding import PartitionSpec as P

D = 6144
BF16 = jnp.bfloat16
F32 = jnp.float32
TILE = 1536
WIDE = 1536
SMALL = 16 * 2**20


def gelu_exact(v):
    return v * 0.5 * (1.0 + lax.erf(v * 0.7071067811865476))


def gelu_slope(v):
    return (
        0.5 * (1.0 + lax.erf(v * 0.7071067811865476))
        + v * jnp.exp(-0.5 * v * v) * 0.3989422804014327
    )


def pairs(first, k):
    out = []
    for core in range(2):
        for z in range(4):
            for y in range(4):
                if (core == 0) == first:
                    to = z * 4 + (y + k) % 4
                else:
                    to = ((z + k) % 4) * 4 + y
                out.append((core * 16 + z * 4 + y, core * 16 + to))
    return out


def shift_row(k):
    return [(r, (r + k) % 4) for r in range(4)]


SWAP = [(0, 1), (1, 0)]


def row_order(where):
    p = lax.broadcasted_iota(jnp.int32, (256, 256), 0)
    q = lax.broadcasted_iota(jnp.int32, (256, 256), 1)
    e, h, i, j = p & 7, (p >> 3) & 1, (p >> 4) & 3, p >> 6
    second = where[0] == 1
    by = (where[1] + jnp.where(second, i, j)) & 3
    bz = (where[2] + jnp.where(second, j, i)) & 3
    return jnp.where(h * 128 + (by * 4 + bz) * 8 + e == q, 1.0, 0.0).astype(BF16)


def reorder(sel, x):
    return jnp.dot(sel, x, preferred_element_type=F32).astype(BF16)


def partials(where, f0, f1, g0, g1, r0, r1, gain, w_in, w_out, *rest):
    outs, (rows_g, g_out, lhs) = rest[:4], rest[4:]

    @pl.when(pl.program_id(0) == 0)
    def _():
        sel = row_order(where)

        def centred(own, other):
            x = jnp.concatenate([own[...], other[...]], axis=0).astype(F32)
            mean = jnp.sum(x, axis=1, keepdims=True) / x.shape[1]
            return ((x - mean) * gain[...]).astype(BF16)

        lhs[0:256, :] = reorder(sel, centred(f0, f1))
        lhs[256:512, :] = reorder(sel, centred(r0, r1))
        rows_g[...] = reorder(sel, jnp.concatenate([g0[...], g1[...]], axis=0))
        a = jnp.broadcast_to(gain[...], (16, gain.shape[1]))
        for k in range(3):
            part = a.astype(BF16)
            lhs[512 + k * 16 : 528 + k * 16, :] = part
            a = a - part.astype(F32)

    product = jnp.dot(lhs[...], w_in[...], preferred_element_type=F32)
    pre, g = product[:512].astype(BF16), product[512:]
    grad = lax.dot_general(
        rows_g[...], w_out[...], (((1,), (1,)), ((), ())), preferred_element_type=F32
    ).astype(BF16)
    for j, o in enumerate(outs):
        for i in range(4):
            at, to = (j * 4 + i) * 16, i * 48
            o[to : to + 16, :] = pre[at : at + 16]
            o[to + 16 : to + 32, :] = pre[256 + at : 256 + at + 16]
            o[to + 32 : to + 48, :] = grad[at : at + 16]
    g_out[...] = (g[32:40] + g[16:24]) + g[0:8]


def stage_sum(own, a, b, c, keep, *sends):
    for i in range(4):
        at = slice(i * 48, i * 48 + 48)
        total = (own[at, :].astype(F32) + a[at, :].astype(F32)) + (
            b[at, :].astype(F32) + c[at, :].astype(F32)
        )
        if i == 0:
            keep[...] = total
        else:
            sends[i - 1][...] = total.astype(BF16)


def merged(width, means, m2, axis):
    mean = jnp.sum(means, axis=axis, keepdims=True) / 16
    gap = means - mean
    var = (
        jnp.sum(m2, axis=axis, keepdims=True)
        + width * jnp.sum(gap * gap, axis=axis, keepdims=True)
    ) / D
    return gap, mean, lax.rsqrt(var + 1e-06)


def activate(width, where, keep, a, b, c, bias, mask, share, out):
    t = pl.program_id(0)
    total = (keep[...] + a[...].astype(F32)) + (b[...].astype(F32) + c[...].astype(F32))
    token = lax.broadcasted_iota(jnp.int32, (8, 128), 0) + (where[1] * 4 + where[2]) * 8
    hot = jnp.where(lax.broadcasted_iota(jnp.int32, (8, 128), 1) == token, 1.0, 0.0)

    def pick(first):
        cols = [
            lax.dot_general(
                hot,
                share[:, first + k, :],
                (((1,), (1,)), ((), ())),
                precision=lax.Precision.HIGHEST,
                preferred_element_type=F32,
            )
            for k in (0, 2, 1, 3)
        ]
        return jnp.concatenate(cols, axis=0)

    gap, _, scale = merged(width, pick(0), pick(4), 1)
    blocks = total.shape[1] // 128
    pre = []
    for r in range(blocks):
        part = total[:32, r * 128 : r * 128 + 128]
        for s in range(16):
            part = part + gap[:, s : s + 1] * share[s, pl.ds(8 + t * blocks + r, 1), :]
        pre.append(part)
    pre = scale * jnp.concatenate(pre, axis=1) + bias[...]
    act = gelu_exact(pre)
    out[0:16, :] = act[:16].astype(BF16)
    out[16:32, :] = (total[32:48] * gelu_slope(pre[:16])).astype(BF16)
    out[32:48, :] = (act[16:32].astype(BF16).astype(F32) * mask[...]).astype(BF16)


def normalise(width, where, own, other, share, gain, out):
    normed = []
    for x, k in ((own, 0), (other, 2)):
        _, mean, scale = merged(width, share[:, k, :], share[:, k + 4, :], 0)
        rows = jnp.concatenate([mean, scale, mean, mean, mean, mean, mean, mean], axis=0)
        cols = jnp.transpose(rows)
        normed.append((x[...].astype(F32) - cols[:, 0:1]) * cols[:, 1:2] * gain[...])
    x = jnp.concatenate(normed, axis=0).astype(BF16)
    rows = jnp.dot(row_order(where), x, preferred_element_type=F32)
    out[...] = jnp.transpose(rows).astype(BF16)


def regroup(b0, b1, b2, b3, forget, retain):
    for i, b in enumerate((b0, b1, b2, b3)):
        at = i * 16
        forget[at : at + 16, :] = b[0:16, :]
        forget[64 + at : 64 + at + 16, :] = b[16:32, :]
        retain[at : at + 16, :] = b[32:48, :]


def saliency_terms(where, b0, b1, b2, b3, normed_t, grad_y, w_in, w_out, out):
    blocks = (b0, b1, b2, b3)
    act = jnp.concatenate([b[0:64, :] for b in blocks], axis=0)
    grad_pre = jnp.concatenate([b[64:128, :] for b in blocks], axis=0)
    grad_in = jnp.dot(normed_t[...], grad_pre, preferred_element_type=F32)
    grad_out = lax.dot_general(
        act, grad_y[...], (((0,), (0,)), ((), ())), preferred_element_type=F32
    )
    term_in = jnp.sum(jnp.abs(w_in[...].astype(F32) * grad_in), axis=0, keepdims=True)
    prod = jnp.abs(w_out[...].astype(F32) * grad_out)
    lanes = (prod[:, 0:128] + prod[:, 128:256]) + prod[:, 256:384]
    term_out = jnp.sum(jnp.transpose(lanes), axis=0, keepdims=True)
    out[...] = jnp.broadcast_to((term_in + term_out)[None], out.shape)


def retain_product(where, b0, b1, b2, b3, w_out, mine, theirs, acc):
    t = pl.program_id(0)
    act = jnp.concatenate([b0[...], b1[...], b2[...], b3[...]], axis=0)
    part = jnp.dot(act, w_out[...], preferred_element_type=F32)

    @pl.when(t == 0)
    def _():
        acc[...] = part

    @pl.when(t > 0)
    def _():
        acc[...] += part

    def store(swap):
        for j in range(4):
            for i in range(4):
                at = (j * 4 + i) * 16
                to = (i * 4 + j if swap else j * 4 + i) * 8
                mine[to : to + 8, :] = acc[at : at + 8, :]
                theirs[to : to + 8, :] = acc[at + 8 : at + 16, :]

    last = t == pl.num_programs(0) - 1

    @pl.when(last & (where[0] == 0))
    def _():
        store(False)

    @pl.when(last & (where[0] == 1))
    def _():
        store(True)


def call(kernel, where, args, outs, scratch=(), steps=6, vmem=None):
    def spec(shape, block, index):
        if block is None:
            return pl.BlockSpec(shape, lambda t, w: (0,) * len(shape))
        return pl.BlockSpec(block, index)

    return pl.pallas_call(
        kernel,
        grid_spec=pltpu.PrefetchScalarGridSpec(
            num_scalar_prefetch=1,
            grid=(steps,),
            in_specs=[spec(a.shape, b, i) for a, b, i in args],
            out_specs=[spec(s, b, i) for s, _, b, i in outs],
            scratch_shapes=list(scratch),
        ),
        out_shape=[jax.ShapeDtypeStruct(s, d) for s, d, _, _ in outs],
        compiler_params=pltpu.CompilerParams(vmem_limit_bytes=vmem),
        cost_estimate=pl.CostEstimate(flops=1, bytes_accessed=1, transcendentals=0),
    )(where, *[a for a, _, _ in args])


def whole(a):
    return (a, None, None)


def by_n(a, tile=TILE):
    return (a, (a.shape[0], tile), lambda t, w: (0, t))


def out_n(rows, n, dtype, tile=TILE):
    return ((rows, n), dtype, (rows, tile), lambda t, w: (0, t))


def drop_where(kernel):
    def inner(where, *refs):
        kernel(*refs)

    return inner


def permutes(parts, first, sign=1):
    return [
        lax.ppermute(parts[k], ("dp", "col"), pairs(first, sign * (k + 1))) for k in range(3)
    ]


def local(
    forget_tokens,
    forget_cotangent,
    forget_labels,
    retain_tokens,
    ln_gain,
    w_in,
    b_in,
    w_out,
    b_out,
    pruned,
):
    core = lax.axis_index("dp")
    row = lax.axis_index("row")
    col = lax.axis_index("col")
    y, z = col % 4, col // 4
    width = w_in.shape[0]
    half = w_in.shape[1] // 2
    steps = half // TILE
    where = jnp.stack([core, y, z]).astype(jnp.int32)
    gain = ln_gain[None, :]

    own_g = forget_cotangent * forget_labels[:, None].astype(BF16)
    other_f = lax.ppermute(forget_tokens, "dp", SWAP)
    other_r = lax.ppermute(retain_tokens, "dp", SWAP)
    other_g = lax.ppermute(own_g, "dp", SWAP)

    w_in_tile = (w_in, (width, TILE), lambda t, w: (0, w[0] * steps + t))
    w_out_tile = (w_out, (TILE, width), lambda t, w: (w[0] * steps + t, 0))
    *parts, grad_y, g_part = call(
        partials,
        where,
        [whole(v) for v in (forget_tokens, other_f, own_g, other_g, retain_tokens, other_r, gain)]
        + [w_in_tile, w_out_tile],
        [out_n(192, half, BF16)] * 4 + [((256, width), BF16, None, None), out_n(8, half, F32)],
        [pltpu.VMEM((560, width), BF16)],
        steps,
    )
    got = permutes(parts[1:], True)

    tokens = jnp.stack([forget_tokens, retain_tokens, other_f, other_r])
    tokens, _ = lax.optimization_barrier((tokens, parts[0]))
    tokens = tokens.astype(F32)
    part_mean = jnp.sum(tokens, axis=2) / width
    centred = tokens - part_mean[..., None]
    part_m2 = jnp.sum(centred * centred, axis=2)
    share = jnp.concatenate([part_mean, part_m2, g_part[0].reshape(half // 128, 128)])
    share = jnp.broadcast_to(share[None], (16,) + share.shape)
    share = lax.all_to_all(share, "col", 0, 0, tiled=True)
    b_half = lax.dynamic_slice_in_dim(b_in, core * half, half, 0)[None, :]
    ids = row * w_in.shape[1] + core * half + jnp.arange(half, dtype=jnp.int32)
    is_pruned = jnp.any(pruned[:, None] == ids[None, :], axis=0)
    keep = jnp.where(is_pruned, 0.0, 1.0)[None, :]

    def wide(kernel, args, outs, extra=(), vmem=SMALL):
        return call(
            drop_where(kernel),
            where,
            [by_n(v, WIDE) for v in args] + [whole(v) for v in extra],
            [out_n(rows, half, kind, WIDE) for rows, kind in outs],
            steps=half // WIDE,
            vmem=vmem,
        )

    sums = wide(stage_sum, [parts[0]] + got, [(48, F32)] + [(48, BF16)] * 3)
    back = permutes(sums[1:], False)
    block = call(
        functools.partial(activate, width),
        where,
        [by_n(v, WIDE) for v in [sums[0]] + back + [b_half, keep]] + [whole(share)],
        [out_n(48, half, BF16, WIDE)],
        steps=half // WIDE,
    )[0]
    near = permutes([block] * 3, False, -1)
    share, _ = lax.optimization_barrier((share, block))
    normed_t = call(
        functools.partial(normalise, width),
        where,
        [whole(forget_tokens), whole(other_f), whole(share), whole(gain)],
        [((width, 256), BF16, None, None)],
        (),
        1,
    )[0]
    near[0], normed_t = lax.optimization_barrier((near[0], normed_t))
    forget, retain = wide(regroup, [block] + near, [(128, BF16), (64, BF16)])
    far = permutes([forget] * 3, True, -1)
    retain, _ = lax.optimization_barrier((retain, far[0]))
    retain_far = permutes([retain] * 3, True, -1)

    terms = call(
        saliency_terms,
        where,
        [by_n(v) for v in [forget] + far] + [whole(normed_t), whole(grad_y), w_in_tile, w_out_tile],
        [((32, 1, half), F32, (32, 1, TILE), lambda t, w: (0, 0, t))],
        (),
        steps,
    )[0]
    terms = lax.all_to_all(terms, ("dp", "col"), 0, 0, tiled=True)

    mine, theirs = call(
        retain_product,
        where,
        [by_n(v) for v in [retain] + retain_far] + [w_out_tile],
        [((128, width), F32, None, None)] * 2,
        [pltpu.VMEM((256, width), F32)],
        steps,
    )
    mine = (mine + lax.ppermute(theirs, "dp", SWAP)).reshape(4, 4, 8, width)

    def for_row(r):
        return lax.dynamic_index_in_dim(mine, (r - y) % 4, 0, keepdims=False)

    from_rows = [lax.ppermute(for_row(row + k), "row", shift_row(k)) for k in (1, 2, 3)]
    terms, _ = lax.optimization_barrier((terms, from_rows[0]))
    saliency = jnp.sum(terms.reshape(2, 16, half), axis=1).reshape(2 * half) / D
    total = for_row(row)
    for part in from_rows:
        total = total + part
    retain_out = (total + b_out).astype(BF16)
    retain_out = lax.dynamic_slice_in_dim(
        jnp.concatenate([retain_out, retain_out], axis=0), (4 - z) % 4, 4, 0
    ).reshape(32, width)
    return (saliency, retain_out)


def solution(mesh):
    in_specs = (
        P("dp", "col"),
        P("dp", "col"),
        P("dp"),
        P("dp", "col"),
        P("col"),
        P("col", "row"),
        P("row"),
        P("row", "col"),
        P("col"),
        P("row"),
    )
    out_specs = (P("row"), P(("dp", "row"), "col"))
    return jax.shard_map(local, mesh=mesh, in_specs=in_specs, out_specs=out_specs, check_vma=False)
```

```python
import functools

import jax
import jax.numpy as jnp
from jax import lax
from jax.experimental import pallas as pl
from jax.experimental.pallas import tpu as pltpu
from jax.sharding import PartitionSpec as P

D = 6144
BF16 = jnp.bfloat16
F32 = jnp.float32
TILE = 1536
WIDE = 3072
SMALL = 16 * 2**20


def gelu_exact(v):
    return v * 0.5 * (1.0 + lax.erf(v * 0.7071067811865476))


def gelu_slope(v):
    return (
        0.5 * (1.0 + lax.erf(v * 0.7071067811865476))
        + v * jnp.exp(-0.5 * v * v) * 0.3989422804014327
    )


def pairs(first, k):
    out = []
    for core in range(2):
        for z in range(4):
            for y in range(4):
                if (core == 0) == first:
                    to = z * 4 + (y + k) % 4
                else:
                    to = ((z + k) % 4) * 4 + y
                out.append((core * 16 + z * 4 + y, core * 16 + to))
    return out


def shift_row(k):
    return [(r, (r + k) % 4) for r in range(4)]


SWAP = [(0, 1), (1, 0)]


def row_order(where):
    p = lax.broadcasted_iota(jnp.int32, (256, 256), 0)
    q = lax.broadcasted_iota(jnp.int32, (256, 256), 1)
    e, h, i, j = p & 7, (p >> 3) & 1, (p >> 4) & 3, p >> 6
    second = where[0] == 1
    by = (where[1] + jnp.where(second, i, j)) & 3
    bz = (where[2] + jnp.where(second, j, i)) & 3
    return jnp.where(h * 128 + (by * 4 + bz) * 8 + e == q, 1.0, 0.0).astype(BF16)


def reorder(sel, x):
    return jnp.dot(sel, x, preferred_element_type=F32).astype(BF16)


def partials(where, f0, f1, g0, g1, r0, r1, l0, l1, gain, w_in, w_out, *rest):
    outs, (rows_g, g_out, lhs) = rest[:4], rest[4:]

    @pl.when(pl.program_id(0) == 0)
    def _():
        sel = row_order(where)

        def centred(own, other):
            x = jnp.concatenate([own[...], other[...]], axis=0).astype(F32)
            mean = jnp.sum(x, axis=1, keepdims=True) / x.shape[1]
            return ((x - mean) * gain[...]).astype(BF16)

        lhs[0:256, :] = reorder(sel, centred(f0, f1))
        lhs[256:512, :] = reorder(sel, centred(r0, r1))
        kept = jnp.concatenate([l0[...], l1[...]], axis=1) == 1
        sel = jnp.where(kept, sel.astype(F32), 0.0).astype(BF16)
        rows_g[...] = reorder(sel, jnp.concatenate([g0[...], g1[...]], axis=0))
        a = jnp.broadcast_to(gain[...], (16, gain.shape[1]))
        for k in range(3):
            part = a.astype(BF16)
            lhs[512 + k * 16 : 528 + k * 16, :] = part
            a = a - part.astype(F32)

    product = jnp.dot(lhs[...], w_in[...], preferred_element_type=F32)
    pre, g = product[:512].astype(BF16), product[512:]
    grad = lax.dot_general(
        rows_g[...], w_out[...], (((1,), (1,)), ((), ())), preferred_element_type=F32
    ).astype(BF16)
    for j, o in enumerate(outs):
        for i in range(4):
            at, to = (j * 4 + i) * 16, i * 48
            o[to : to + 16, :] = pre[at : at + 16]
            o[to + 16 : to + 32, :] = pre[256 + at : 256 + at + 16]
            o[to + 32 : to + 48, :] = grad[at : at + 16]
    g_out[...] = (g[32:40] + g[16:24]) + g[0:8]


def stage_sum(own, a, b, c, keep, *sends):
    for i in range(4):
        at = slice(i * 48, i * 48 + 48)
        total = (own[at, :].astype(F32) + a[at, :].astype(F32)) + (
            b[at, :].astype(F32) + c[at, :].astype(F32)
        )
        if i == 0:
            keep[...] = total
        else:
            sends[i - 1][...] = total.astype(BF16)


def merged(width, means, m2, axis):
    mean = jnp.sum(means, axis=axis, keepdims=True) / 16
    gap = means - mean
    var = (
        jnp.sum(m2, axis=axis, keepdims=True)
        + width * jnp.sum(gap * gap, axis=axis, keepdims=True)
    ) / D
    return gap, mean, lax.rsqrt(var + 1e-06)


def activate(width, where, keep, a, b, c, bias, mask, share, out):
    t = pl.program_id(0)
    total = (keep[...] + a[...].astype(F32)) + (b[...].astype(F32) + c[...].astype(F32))
    token = lax.broadcasted_iota(jnp.int32, (8, 128), 0) + (where[1] * 4 + where[2]) * 8
    hot = jnp.where(lax.broadcasted_iota(jnp.int32, (8, 128), 1) == token, 1.0, 0.0)

    def pick(first):
        cols = [
            lax.dot_general(
                hot,
                share[:, first + k, :],
                (((1,), (1,)), ((), ())),
                precision=lax.Precision.HIGHEST,
                preferred_element_type=F32,
            )
            for k in (0, 2, 1, 3)
        ]
        return jnp.concatenate(cols, axis=0)

    gap, _, scale = merged(width, pick(0), pick(4), 1)
    blocks = total.shape[1] // 128
    pre = []
    for r in range(blocks):
        part = total[:32, r * 128 : r * 128 + 128]
        for s in range(16):
            part = part + gap[:, s : s + 1] * share[s, pl.ds(8 + t * blocks + r, 1), :]
        pre.append(part)
    pre = scale * jnp.concatenate(pre, axis=1) + bias[...]
    act = gelu_exact(pre)
    out[0:16, :] = act[:16].astype(BF16)
    out[16:32, :] = (total[32:48] * gelu_slope(pre[:16])).astype(BF16)
    out[32:48, :] = (act[16:32].astype(BF16).astype(F32) * mask[...]).astype(BF16)


def normalise(width, where, own, other, share, gain, out):
    normed = []
    for x, k in ((own, 0), (other, 2)):
        _, mean, scale = merged(width, share[:, k, :], share[:, k + 4, :], 0)
        rows = jnp.concatenate([mean, scale, mean, mean, mean, mean, mean, mean], axis=0)
        cols = jnp.transpose(rows)
        normed.append((x[...].astype(F32) - cols[:, 0:1]) * cols[:, 1:2] * gain[...])
    x = jnp.concatenate(normed, axis=0).astype(BF16)
    rows = jnp.dot(row_order(where), x, preferred_element_type=F32)
    out[...] = jnp.transpose(rows).astype(BF16)


def regroup(b0, b1, b2, b3, forget, retain):
    for i, b in enumerate((b0, b1, b2, b3)):
        at = i * 16
        forget[at : at + 16, :] = b[0:16, :]
        forget[64 + at : 64 + at + 16, :] = b[16:32, :]
        retain[at : at + 16, :] = b[32:48, :]


def saliency_terms(where, b0, b1, b2, b3, normed_t, grad_y, w_in, w_out, out):
    blocks = (b0, b1, b2, b3)
    act = jnp.concatenate([b[0:64, :] for b in blocks], axis=0)
    grad_pre = jnp.concatenate([b[64:128, :] for b in blocks], axis=0)
    grad_in = jnp.dot(normed_t[...], grad_pre, preferred_element_type=F32)
    grad_out = lax.dot_general(
        act, grad_y[...], (((0,), (0,)), ((), ())), preferred_element_type=F32
    )
    term_in = jnp.sum(jnp.abs(w_in[...].astype(F32) * grad_in), axis=0, keepdims=True)
    prod = jnp.abs(w_out[...].astype(F32) * grad_out)
    lanes = (prod[:, 0:128] + prod[:, 128:256]) + prod[:, 256:384]
    term_out = jnp.sum(jnp.transpose(lanes), axis=0, keepdims=True)
    out[...] = jnp.broadcast_to((term_in + term_out)[None], out.shape)


def retain_product(where, b0, b1, b2, b3, w_out, mine, theirs, acc):
    t = pl.program_id(0)
    act = jnp.concatenate([b0[...], b1[...], b2[...], b3[...]], axis=0)
    part = jnp.dot(act, w_out[...], preferred_element_type=F32)

    @pl.when(t == 0)
    def _():
        acc[...] = part

    @pl.when(t > 0)
    def _():
        acc[...] += part

    def store(swap):
        for j in range(4):
            for i in range(4):
                at = (j * 4 + i) * 16
                to = (i * 4 + j if swap else j * 4 + i) * 8
                mine[to : to + 8, :] = acc[at : at + 8, :]
                theirs[to : to + 8, :] = acc[at + 8 : at + 16, :]

    last = t == pl.num_programs(0) - 1

    @pl.when(last & (where[0] == 0))
    def _():
        store(False)

    @pl.when(last & (where[0] == 1))
    def _():
        store(True)


def call(kernel, where, args, outs, scratch=(), steps=6, vmem=28 * 2**20):
    def spec(shape, block, index):
        if block is None:
            return pl.BlockSpec(shape, lambda t, w: (0,) * len(shape))
        return pl.BlockSpec(block, index)

    return pl.pallas_call(
        kernel,
        grid_spec=pltpu.PrefetchScalarGridSpec(
            num_scalar_prefetch=1,
            grid=(steps,),
            in_specs=[spec(a.shape, b, i) for a, b, i in args],
            out_specs=[spec(s, b, i) for s, _, b, i in outs],
            scratch_shapes=list(scratch),
        ),
        out_shape=[jax.ShapeDtypeStruct(s, d) for s, d, _, _ in outs],
        compiler_params=pltpu.CompilerParams(vmem_limit_bytes=vmem),
        cost_estimate=pl.CostEstimate(flops=1, bytes_accessed=1, transcendentals=0),
    )(where, *[a for a, _, _ in args])


def whole(a):
    return (a, None, None)


def by_n(a, tile=TILE):
    return (a, (a.shape[0], tile), lambda t, w: (0, t))


def out_n(rows, n, dtype, tile=TILE):
    return ((rows, n), dtype, (rows, tile), lambda t, w: (0, t))


def drop_where(kernel):
    def inner(where, *refs):
        kernel(*refs)

    return inner


def permutes(parts, first, sign=1):
    return [
        lax.ppermute(parts[k], ("dp", "col"), pairs(first, sign * (k + 1))) for k in range(3)
    ]


def local(
    forget_tokens,
    forget_cotangent,
    forget_labels,
    retain_tokens,
    ln_gain,
    w_in,
    b_in,
    w_out,
    b_out,
    pruned,
):
    core = lax.axis_index("dp")
    row = lax.axis_index("row")
    col = lax.axis_index("col")
    y, z = col % 4, col // 4
    width = w_in.shape[0]
    half = w_in.shape[1] // 2
    steps = half // TILE
    where = jnp.stack([core, y, z]).astype(jnp.int32)
    gain = ln_gain[None, :]

    labels = forget_labels[None, :]
    other_f = lax.ppermute(forget_tokens, "dp", SWAP)
    other_r = lax.ppermute(retain_tokens, "dp", SWAP)
    other_g = lax.ppermute(forget_cotangent, "dp", SWAP)
    other_labels = lax.ppermute(labels, "dp", SWAP)

    w_in_tile = (w_in, (width, TILE), lambda t, w: (0, w[0] * steps + t))
    w_out_tile = (w_out, (TILE, width), lambda t, w: (w[0] * steps + t, 0))
    *parts, grad_y, g_part = call(
        partials,
        where,
        [whole(v) for v in (forget_tokens, other_f, forget_cotangent, other_g)]
        + [whole(v) for v in (retain_tokens, other_r, labels, other_labels, gain)]
        + [w_in_tile, w_out_tile],
        [out_n(192, half, BF16)] * 4 + [((256, width), BF16, None, None), out_n(8, half, F32)],
        [pltpu.VMEM((560, width), BF16)],
        steps,
        None,
    )
    got = permutes(parts[1:], True)

    tokens = jnp.stack([forget_tokens, retain_tokens, other_f, other_r])
    tokens, _ = lax.optimization_barrier((tokens, parts[0]))
    tokens = tokens.astype(F32)
    part_mean = jnp.sum(tokens, axis=2) / width
    centred = tokens - part_mean[..., None]
    part_m2 = jnp.sum(centred * centred, axis=2)
    share = jnp.concatenate([part_mean, part_m2, g_part[0].reshape(half // 128, 128)])
    share = jnp.broadcast_to(share[None], (16,) + share.shape)
    share = lax.all_to_all(share, "col", 0, 0, tiled=True)
    b_half = lax.dynamic_slice_in_dim(b_in, core * half, half, 0)[None, :]
    ids = row * w_in.shape[1] + core * half + jnp.arange(half, dtype=jnp.int32)
    is_pruned = jnp.any(pruned[:, None] == ids[None, :], axis=0)
    keep = jnp.where(is_pruned, 0.0, 1.0)[None, :]

    def wide(kernel, args, outs, extra=(), vmem=SMALL):
        return call(
            drop_where(kernel),
            where,
            [by_n(v, WIDE) for v in args] + [whole(v) for v in extra],
            [out_n(rows, half, kind, WIDE) for rows, kind in outs],
            steps=half // WIDE,
            vmem=vmem,
        )

    sums = wide(stage_sum, [parts[0]] + got, [(48, F32)] + [(48, BF16)] * 3)
    back = permutes(sums[1:], False)
    block = call(
        functools.partial(activate, width),
        where,
        [by_n(v, WIDE) for v in [sums[0]] + back + [b_half, keep]] + [whole(share)],
        [out_n(48, half, BF16, WIDE)],
        steps=half // WIDE,
    )[0]
    near = permutes([block] * 3, False, -1)
    share, _ = lax.optimization_barrier((share, block))
    normed_t = call(
        functools.partial(normalise, width),
        where,
        [whole(forget_tokens), whole(other_f), whole(share), whole(gain)],
        [((width, 256), BF16, None, None)],
        (),
        1,
    )[0]
    near[0], normed_t = lax.optimization_barrier((near[0], normed_t))
    forget, retain = wide(regroup, [block] + near, [(128, BF16), (64, BF16)])
    far = permutes([forget] * 3, True, -1)
    first, last, _ = lax.optimization_barrier((w_in, w_out, forget))
    first = lax.dynamic_slice_in_dim(first, core * half, half, 1)
    last = lax.dynamic_slice_in_dim(last, core * half, half, 0)
    retain, far[0], first, last = lax.optimization_barrier((retain, far[0], first, last))
    w_in_tile = (first, (width, TILE), lambda t, w: (0, t))
    w_out_tile = (last, (TILE, width), lambda t, w: (t, 0))
    retain_far = permutes([retain] * 3, True, -1)

    terms = call(
        saliency_terms,
        where,
        [by_n(v) for v in [forget] + far] + [whole(normed_t), whole(grad_y), w_in_tile, w_out_tile],
        [((32, 1, half), F32, (32, 1, TILE), lambda t, w: (0, 0, t))],
        (),
        steps,
    )[0]
    terms = lax.all_to_all(terms, ("dp", "col"), 0, 0, tiled=True)

    mine, theirs = call(
        retain_product,
        where,
        [by_n(v) for v in [retain] + retain_far] + [w_out_tile],
        [((128, width), F32, None, None)] * 2,
        [pltpu.VMEM((256, width), F32)],
        steps,
    )
    mine = (mine + lax.ppermute(theirs, "dp", SWAP)).reshape(4, 4, 8, width)

    def for_row(r):
        return lax.dynamic_index_in_dim(mine, (r - y) % 4, 0, keepdims=False)

    from_rows = [lax.ppermute(for_row(row + k), "row", shift_row(k)) for k in (1, 2, 3)]
    terms, _ = lax.optimization_barrier((terms, from_rows[0]))
    saliency = jnp.sum(terms.reshape(2, 16, half), axis=1).reshape(2 * half) / D
    total = for_row(row)
    for part in from_rows:
        total = total + part
    retain_out = (total + b_out).astype(BF16)
    retain_out = lax.dynamic_slice_in_dim(
        jnp.concatenate([retain_out, retain_out], axis=0), (4 - z) % 4, 4, 0
    ).reshape(32, width)
    return (saliency, retain_out)


def solution(mesh):
    in_specs = (
        P("dp", "col"),
        P("dp", "col"),
        P("dp"),
        P("dp", "col"),
        P("col"),
        P("col", "row"),
        P("row"),
        P("row", "col"),
        P("col"),
        P("row"),
    )
    out_specs = (P("row"), P(("dp", "row"), "col"))
    return jax.shard_map(local, mesh=mesh, in_specs=in_specs, out_specs=out_specs, check_vma=False)
```

```python
import functools

import jax
import jax.numpy as jnp
from jax import lax
from jax.experimental import pallas as pl
from jax.experimental.pallas import tpu as pltpu
from jax.sharding import PartitionSpec as P

D = 6144
BF16 = jnp.bfloat16
F32 = jnp.float32
TILE = 1536
WIDE = 3072
SMALL = 16 * 2**20


def gelu_exact(v):
    return v * 0.5 * (1.0 + lax.erf(v * 0.7071067811865476))


def gelu_slope(v):
    return (
        0.5 * (1.0 + lax.erf(v * 0.7071067811865476))
        + v * jnp.exp(-0.5 * v * v) * 0.3989422804014327
    )


def pairs(first, k):
    out = []
    for core in range(2):
        for z in range(4):
            for y in range(4):
                if (core == 0) == first:
                    to = z * 4 + (y + k) % 4
                else:
                    to = ((z + k) % 4) * 4 + y
                out.append((core * 16 + z * 4 + y, core * 16 + to))
    return out


def shift_row(k):
    return [(r, (r + k) % 4) for r in range(4)]


SWAP = [(0, 1), (1, 0)]


def row_order(where):
    p = lax.broadcasted_iota(jnp.int32, (256, 256), 0)
    q = lax.broadcasted_iota(jnp.int32, (256, 256), 1)
    e, h, i, j = p & 7, (p >> 3) & 1, (p >> 4) & 3, p >> 6
    second = where[0] == 1
    by = (where[1] + jnp.where(second, i, j)) & 3
    bz = (where[2] + jnp.where(second, j, i)) & 3
    return jnp.where(h * 128 + (by * 4 + bz) * 8 + e == q, 1.0, 0.0).astype(BF16)


def reorder(sel, x):
    return jnp.dot(sel, x, preferred_element_type=F32).astype(BF16)


def partials(where, f0, f1, g0, g1, r0, r1, l0, l1, gain, w_in, w_out, *rest):
    outs, (rows_g, g_out, lhs) = rest[:4], rest[4:]

    @pl.when(pl.program_id(0) == 0)
    def _():
        sel = row_order(where)

        def centred(own, other):
            x = jnp.concatenate([own[...], other[...]], axis=0).astype(F32)
            mean = jnp.sum(x, axis=1, keepdims=True) / x.shape[1]
            return ((x - mean) * gain[...][None, :]).astype(BF16)

        lhs[0:256, :] = reorder(sel, centred(f0, f1))
        lhs[256:512, :] = reorder(sel, centred(r0, r1))
        kept = jnp.concatenate([l0[...], l1[...]], axis=1) == 1
        sel = jnp.where(kept, sel.astype(F32), 0.0).astype(BF16)
        rows_g[...] = reorder(sel, jnp.concatenate([g0[...], g1[...]], axis=0))
        a = jnp.broadcast_to(gain[...][None, :], (16, gain.shape[0]))
        for k in range(3):
            part = a.astype(BF16)
            lhs[512 + k * 16 : 528 + k * 16, :] = part
            a = a - part.astype(F32)

    product = jnp.dot(lhs[...], w_in[...], preferred_element_type=F32)
    pre, g = product[:512].astype(BF16), product[512:]
    grad = lax.dot_general(
        rows_g[...], w_out[...], (((1,), (1,)), ((), ())), preferred_element_type=F32
    ).astype(BF16)
    for j, o in enumerate(outs):
        for i in range(4):
            at, to = (j * 4 + i) * 16, i * 48
            o[to : to + 16, :] = pre[at : at + 16]
            o[to + 16 : to + 32, :] = pre[256 + at : 256 + at + 16]
            o[to + 32 : to + 48, :] = grad[at : at + 16]
    g_out[...] = (g[32:40] + g[16:24]) + g[0:8]


def stage_sum(own, a, b, c, keep, *sends):
    for i in range(4):
        at = slice(i * 48, i * 48 + 48)
        total = (own[at, :].astype(F32) + a[at, :].astype(F32)) + (
            b[at, :].astype(F32) + c[at, :].astype(F32)
        )
        if i == 0:
            keep[...] = total
        else:
            sends[i - 1][...] = total.astype(BF16)


def merged(width, means, m2, axis):
    mean = jnp.sum(means, axis=axis, keepdims=True) / 16
    gap = means - mean
    var = (
        jnp.sum(m2, axis=axis, keepdims=True)
        + width * jnp.sum(gap * gap, axis=axis, keepdims=True)
    ) / D
    return gap, mean, lax.rsqrt(var + 1e-06)


def activate(width, where, keep, a, b, c, bias, mask, share, out):
    t = pl.program_id(0)
    total = (keep[...] + a[...].astype(F32)) + (b[...].astype(F32) + c[...].astype(F32))
    token = lax.broadcasted_iota(jnp.int32, (8, 128), 0) + (where[1] * 4 + where[2]) * 8
    hot = jnp.where(lax.broadcasted_iota(jnp.int32, (8, 128), 1) == token, 1.0, 0.0)

    def pick(first):
        cols = [
            lax.dot_general(
                hot,
                share[:, first + k, :],
                (((1,), (1,)), ((), ())),
                precision=lax.Precision.HIGHEST,
                preferred_element_type=F32,
            )
            for k in (0, 2, 1, 3)
        ]
        return jnp.concatenate(cols, axis=0)

    gap, _, scale = merged(width, pick(0), pick(4), 1)
    blocks = total.shape[1] // 128
    pre = []
    for r in range(blocks):
        part = total[:32, r * 128 : r * 128 + 128]
        for s in range(16):
            part = part + gap[:, s : s + 1] * share[s, pl.ds(8 + t * blocks + r, 1), :]
        pre.append(part)
    pre = scale * jnp.concatenate(pre, axis=1) + bias[...]
    act = gelu_exact(pre)
    out[0:16, :] = act[:16].astype(BF16)
    out[16:32, :] = (total[32:48] * gelu_slope(pre[:16])).astype(BF16)
    out[32:48, :] = (act[16:32].astype(BF16).astype(F32) * mask[...]).astype(BF16)


def normalise(width, where, own, other, share, gain, out):
    normed = []
    for x, k in ((own, 0), (other, 2)):
        _, mean, scale = merged(width, share[:, k, :], share[:, k + 4, :], 0)
        rows = jnp.concatenate([mean, scale, mean, mean, mean, mean, mean, mean], axis=0)
        cols = jnp.transpose(rows)
        normed.append((x[...].astype(F32) - cols[:, 0:1]) * cols[:, 1:2] * gain[...][None, :])
    x = jnp.concatenate(normed, axis=0).astype(BF16)
    rows = jnp.dot(row_order(where), x, preferred_element_type=F32)
    out[...] = jnp.transpose(rows).astype(BF16)


def regroup(b0, b1, b2, b3, forget, retain):
    for i, b in enumerate((b0, b1, b2, b3)):
        at = i * 16
        forget[at : at + 16, :] = b[0:16, :]
        forget[64 + at : 64 + at + 16, :] = b[16:32, :]
        retain[at : at + 16, :] = b[32:48, :]


def saliency_terms(where, b0, b1, b2, b3, normed_t, grad_y, w_in, w_out, out):
    blocks = (b0, b1, b2, b3)
    act = jnp.concatenate([b[0:64, :] for b in blocks], axis=0)
    grad_pre = jnp.concatenate([b[64:128, :] for b in blocks], axis=0)
    grad_in = jnp.dot(normed_t[...], grad_pre, preferred_element_type=F32)
    grad_out = lax.dot_general(
        act, grad_y[...], (((0,), (0,)), ((), ())), preferred_element_type=F32
    )
    term_in = jnp.sum(jnp.abs(w_in[...].astype(F32) * grad_in), axis=0, keepdims=True)
    prod = jnp.abs(w_out[...].astype(F32) * grad_out)
    lanes = (prod[:, 0:128] + prod[:, 128:256]) + prod[:, 256:384]
    term_out = jnp.sum(jnp.transpose(lanes), axis=0, keepdims=True)
    out[...] = jnp.broadcast_to((term_in + term_out)[None], out.shape)


def retain_product(where, b0, b1, b2, b3, w_out, mine, theirs, acc):
    t = pl.program_id(0)
    act = jnp.concatenate([b0[...], b1[...], b2[...], b3[...]], axis=0)
    part = jnp.dot(act, w_out[...], preferred_element_type=F32)

    @pl.when(t == 0)
    def _():
        acc[...] = part

    @pl.when(t > 0)
    def _():
        acc[...] += part

    def store(swap):
        for j in range(4):
            for i in range(4):
                at = (j * 4 + i) * 16
                to = (i * 4 + j if swap else j * 4 + i) * 8
                mine[to : to + 8, :] = acc[at : at + 8, :]
                theirs[to : to + 8, :] = acc[at + 8 : at + 16, :]

    last = t == pl.num_programs(0) - 1

    @pl.when(last & (where[0] == 0))
    def _():
        store(False)

    @pl.when(last & (where[0] == 1))
    def _():
        store(True)


def call(kernel, where, args, outs, scratch=(), steps=6, vmem=28 * 2**20):
    def spec(shape, block, index):
        if block is None:
            return pl.BlockSpec(shape, lambda t, w: (0,) * len(shape))
        return pl.BlockSpec(block, index)

    return pl.pallas_call(
        kernel,
        grid_spec=pltpu.PrefetchScalarGridSpec(
            num_scalar_prefetch=1,
            grid=(steps,),
            in_specs=[spec(a.shape, b, i) for a, b, i in args],
            out_specs=[spec(s, b, i) for s, _, b, i in outs],
            scratch_shapes=list(scratch),
        ),
        out_shape=[jax.ShapeDtypeStruct(s, d) for s, d, _, _ in outs],
        compiler_params=pltpu.CompilerParams(vmem_limit_bytes=vmem),
        cost_estimate=pl.CostEstimate(flops=1, bytes_accessed=1, transcendentals=0),
    )(where, *[a for a, _, _ in args])


def whole(a):
    return (a, None, None)


def by_n(a, tile=TILE):
    return (a, (a.shape[0], tile), lambda t, w: (0, t))


def out_n(rows, n, dtype, tile=TILE):
    return ((rows, n), dtype, (rows, tile), lambda t, w: (0, t))


def drop_where(kernel):
    def inner(where, *refs):
        kernel(*refs)

    return inner


def permutes(parts, first, sign=1):
    return [
        lax.ppermute(parts[k], ("dp", "col"), pairs(first, sign * (k + 1))) for k in range(3)
    ]


def local(
    forget_tokens,
    forget_cotangent,
    forget_labels,
    retain_tokens,
    ln_gain,
    w_in,
    b_in,
    w_out,
    b_out,
    pruned,
):
    core = lax.axis_index("dp")
    row = lax.axis_index("row")
    col = lax.axis_index("col")
    y, z = col % 4, col // 4
    width = w_in.shape[0]
    half = w_in.shape[1] // 2
    steps = half // TILE
    where = jnp.stack([core, y, z]).astype(jnp.int32)
    gain = ln_gain

    labels = forget_labels[None, :]
    other_f = lax.ppermute(forget_tokens, "dp", SWAP)
    other_r = lax.ppermute(retain_tokens, "dp", SWAP)
    other_g = lax.ppermute(forget_cotangent, "dp", SWAP)
    other_labels = lax.ppermute(labels, "dp", SWAP)

    w_in_tile = (w_in, (width, TILE), lambda t, w: (0, w[0] * steps + t))
    w_out_tile = (w_out, (TILE, width), lambda t, w: (w[0] * steps + t, 0))
    *parts, grad_y, g_part = call(
        partials,
        where,
        [whole(v) for v in (forget_tokens, other_f, forget_cotangent, other_g)]
        + [whole(v) for v in (retain_tokens, other_r, labels, other_labels, gain)]
        + [w_in_tile, w_out_tile],
        [out_n(192, half, BF16)] * 4 + [((256, width), BF16, None, None), out_n(8, half, F32)],
        [pltpu.VMEM((560, width), BF16)],
        steps,
        None,
    )
    got = permutes(parts[1:], True)

    tokens = jnp.stack([forget_tokens, retain_tokens, other_f, other_r])
    tokens, _ = lax.optimization_barrier((tokens, parts[0]))
    tokens = tokens.astype(F32)
    part_mean = jnp.sum(tokens, axis=2) / width
    centred = tokens - part_mean[..., None]
    part_m2 = jnp.sum(centred * centred, axis=2)
    share = jnp.concatenate([part_mean, part_m2, g_part[0].reshape(half // 128, 128)])
    share = jnp.broadcast_to(share[None], (16,) + share.shape)
    share = lax.all_to_all(share, "col", 0, 0, tiled=True)
    b_half = lax.dynamic_slice_in_dim(b_in, core * half, half, 0)[None, :]
    ids = row * w_in.shape[1] + core * half + jnp.arange(half, dtype=jnp.int32)
    is_pruned = jnp.any(pruned[:, None] == ids[None, :], axis=0)
    keep = jnp.where(is_pruned, 0.0, 1.0)[None, :]

    def wide(kernel, args, outs, extra=(), vmem=SMALL):
        return call(
            drop_where(kernel),
            where,
            [by_n(v, WIDE) for v in args] + [whole(v) for v in extra],
            [out_n(rows, half, kind, WIDE) for rows, kind in outs],
            steps=half // WIDE,
            vmem=vmem,
        )

    sums = wide(stage_sum, [parts[0]] + got, [(48, F32)] + [(48, BF16)] * 3)
    back = permutes(sums[1:], False)
    block = call(
        functools.partial(activate, width),
        where,
        [by_n(v, WIDE) for v in [sums[0]] + back + [b_half, keep]] + [whole(share)],
        [out_n(48, half, BF16, WIDE)],
        steps=half // WIDE,
    )[0]
    near = permutes([block] * 3, False, -1)
    share, _ = lax.optimization_barrier((share, block))
    normed_t = call(
        functools.partial(normalise, width),
        where,
        [whole(forget_tokens), whole(other_f), whole(share), whole(gain)],
        [((width, 256), BF16, None, None)],
        (),
        1,
    )[0]
    near[0], normed_t = lax.optimization_barrier((near[0], normed_t))
    forget, retain = wide(regroup, [block] + near, [(128, BF16), (64, BF16)])
    far = permutes([forget] * 3, True, -1)
    first, last, _ = lax.optimization_barrier((w_in, w_out, forget))
    first = lax.dynamic_slice_in_dim(first, core * half, half, 1)
    last = lax.dynamic_slice_in_dim(last, core * half, half, 0)
    retain, first = lax.optimization_barrier((retain, first))
    second, last = lax.optimization_barrier((retain, last))
    far[0], first, last = lax.optimization_barrier((far[0], first, last))
    w_in_tile = (first, (width, TILE), lambda t, w: (0, t))
    w_out_tile = (last, (TILE, width), lambda t, w: (t, 0))
    retain_far = permutes([retain, second, second], True, -1)

    terms = call(
        saliency_terms,
        where,
        [by_n(v) for v in [forget] + far] + [whole(normed_t), whole(grad_y), w_in_tile, w_out_tile],
        [((32, 1, half), F32, (32, 1, TILE), lambda t, w: (0, 0, t))],
        (),
        steps,
    )[0]
    retain_far[0], _ = lax.optimization_barrier((retain_far[0], terms))
    terms = lax.all_to_all(terms, ("dp", "col"), 0, 0, tiled=True)

    mine, theirs = call(
        retain_product,
        where,
        [by_n(v) for v in [retain] + retain_far] + [w_out_tile],
        [((128, width), F32, None, None)] * 2,
        [pltpu.VMEM((256, width), F32)],
        steps,
    )
    mine = (mine + lax.ppermute(theirs, "dp", SWAP)).reshape(4, 4, 8, width)

    def for_row(r):
        return lax.dynamic_index_in_dim(mine, (r - y) % 4, 0, keepdims=False)

    from_rows = [lax.ppermute(for_row(row + k), "row", shift_row(k)) for k in (1, 2, 3)]
    terms, _ = lax.optimization_barrier((terms, from_rows[0]))
    saliency = jnp.sum(terms.reshape(2, 16, half), axis=1).reshape(2 * half) / D
    from_rows[1], saliency = lax.optimization_barrier((from_rows[1], saliency))
    total = for_row(row)
    for part in from_rows:
        total = total + part
    retain_out = (total + b_out).astype(BF16)
    retain_out = lax.dynamic_slice_in_dim(
        jnp.concatenate([retain_out, retain_out], axis=0), (4 - z) % 4, 4, 0
    ).reshape(32, width)
    return (saliency, retain_out)


def solution(mesh):
    in_specs = (
        P("dp", "col"),
        P("dp", "col"),
        P("dp"),
        P("dp", "col"),
        P("col"),
        P("col", "row"),
        P("row"),
        P("row", "col"),
        P("col"),
        P("row"),
    )
    out_specs = (P("row"), P(("dp", "row"), "col"))
    return jax.shard_map(local, mesh=mesh, in_specs=in_specs, out_specs=out_specs, check_vma=False)
```

```python
import functools

import jax
import jax.numpy as jnp
from jax import lax
from jax.experimental import pallas as pl
from jax.experimental.pallas import tpu as pltpu
from jax.sharding import PartitionSpec as P

D = 6144
BF16 = jnp.bfloat16
F32 = jnp.float32
TILE = 1536
WIDE = 3072
SMALL = 16 * 2**20


def gelu_exact(v):
    return v * 0.5 * (1.0 + lax.erf(v * 0.7071067811865476))


def gelu_slope(v):
    return (
        0.5 * (1.0 + lax.erf(v * 0.7071067811865476))
        + v * jnp.exp(-0.5 * v * v) * 0.3989422804014327
    )


def pairs(first, k):
    out = []
    for core in range(2):
        for z in range(4):
            for y in range(4):
                if (core == 0) == first:
                    to = z * 4 + (y + k) % 4
                else:
                    to = ((z + k) % 4) * 4 + y
                out.append((core * 16 + z * 4 + y, core * 16 + to))
    return out


def shift_row(k):
    return [(r, (r + k) % 4) for r in range(4)]


SWAP = [(0, 1), (1, 0)]


def row_order(where):
    p = lax.broadcasted_iota(jnp.int32, (256, 256), 0)
    q = lax.broadcasted_iota(jnp.int32, (256, 256), 1)
    e, h, i, j = p & 7, (p >> 3) & 1, (p >> 4) & 3, p >> 6
    second = where[0] == 1
    by = (where[1] + jnp.where(second, i, j)) & 3
    bz = (where[2] + jnp.where(second, j, i)) & 3
    return jnp.where(h * 128 + (by * 4 + bz) * 8 + e == q, 1.0, 0.0).astype(BF16)


def reorder(sel, x):
    return jnp.dot(sel, x, preferred_element_type=F32).astype(BF16)


def partials(where, f0, f1, g0, g1, r0, r1, l0, l1, gain, w_in, w_out, *rest):
    outs, (rows_g, g_out, lhs) = rest[:4], rest[4:]

    @pl.when(pl.program_id(0) == 0)
    def _():
        sel = row_order(where)

        def centred(own, other):
            x = jnp.concatenate([own[...], other[...]], axis=0).astype(F32)
            mean = jnp.sum(x, axis=1, keepdims=True) / x.shape[1]
            return ((x - mean) * gain[...][None, :]).astype(BF16)

        lhs[0:256, :] = reorder(sel, centred(f0, f1))
        lhs[256:512, :] = reorder(sel, centred(r0, r1))
        kept = jnp.concatenate([l0[...], l1[...]], axis=1) == 1
        sel = jnp.where(kept, sel.astype(F32), 0.0).astype(BF16)
        rows_g[...] = reorder(sel, jnp.concatenate([g0[...], g1[...]], axis=0))
        a = jnp.broadcast_to(gain[...][None, :], (16, gain.shape[0]))
        for k in range(3):
            part = a.astype(BF16)
            lhs[512 + k * 16 : 528 + k * 16, :] = part
            a = a - part.astype(F32)

    product = jnp.dot(lhs[...], w_in[...], preferred_element_type=F32)
    pre, g = product[:512].astype(BF16), product[512:]
    grad = lax.dot_general(
        rows_g[...], w_out[...], (((1,), (1,)), ((), ())), preferred_element_type=F32
    ).astype(BF16)
    for j, o in enumerate(outs):
        for i in range(4):
            at, to = (j * 4 + i) * 16, i * 48
            o[to : to + 16, :] = pre[at : at + 16]
            o[to + 16 : to + 32, :] = pre[256 + at : 256 + at + 16]
            o[to + 32 : to + 48, :] = grad[at : at + 16]
    g_out[...] = (g[32:40] + g[16:24]) + g[0:8]


def stage_sum(own, a, b, c, keep, *sends):
    for i in range(4):
        at = slice(i * 48, i * 48 + 48)
        total = (own[at, :].astype(F32) + a[at, :].astype(F32)) + (
            b[at, :].astype(F32) + c[at, :].astype(F32)
        )
        if i == 0:
            keep[...] = total
        else:
            sends[i - 1][...] = total.astype(BF16)


def merged(width, means, m2, axis):
    mean = jnp.sum(means, axis=axis, keepdims=True) / 16
    gap = means - mean
    var = (
        jnp.sum(m2, axis=axis, keepdims=True)
        + width * jnp.sum(gap * gap, axis=axis, keepdims=True)
    ) / D
    return gap, mean, lax.rsqrt(var + 1e-06)


def activate(width, where, keep, a, b, c, bias, mask, share, out):
    t = pl.program_id(0)
    total = (keep[...] + a[...].astype(F32)) + (b[...].astype(F32) + c[...].astype(F32))
    token = lax.broadcasted_iota(jnp.int32, (8, 128), 0) + (where[1] * 4 + where[2]) * 8
    hot = jnp.where(lax.broadcasted_iota(jnp.int32, (8, 128), 1) == token, 1.0, 0.0)

    def pick(first):
        cols = [
            lax.dot_general(
                hot,
                share[:, first + k, :],
                (((1,), (1,)), ((), ())),
                precision=lax.Precision.HIGHEST,
                preferred_element_type=F32,
            )
            for k in (0, 2, 1, 3)
        ]
        return jnp.concatenate(cols, axis=0)

    gap, _, scale = merged(width, pick(0), pick(4), 1)
    blocks = total.shape[1] // 128
    pre = []
    for r in range(blocks):
        part = total[:32, r * 128 : r * 128 + 128]
        for s in range(16):
            part = part + gap[:, s : s + 1] * share[s, pl.ds(8 + t * blocks + r, 1), :]
        pre.append(part)
    pre = scale * jnp.concatenate(pre, axis=1) + bias[...]
    act = gelu_exact(pre)
    out[0:16, :] = act[:16].astype(BF16)
    out[16:32, :] = (total[32:48] * gelu_slope(pre[:16])).astype(BF16)
    out[32:48, :] = (act[16:32].astype(BF16).astype(F32) * mask[...]).astype(BF16)


def normalise(width, where, own, other, share, gain, out):
    normed = []
    for x, k in ((own, 0), (other, 2)):
        _, mean, scale = merged(width, share[:, k, :], share[:, k + 4, :], 0)
        rows = jnp.concatenate([mean, scale, mean, mean, mean, mean, mean, mean], axis=0)
        cols = jnp.transpose(rows)
        normed.append((x[...].astype(F32) - cols[:, 0:1]) * cols[:, 1:2] * gain[...][None, :])
    x = jnp.concatenate(normed, axis=0).astype(BF16)
    rows = jnp.dot(row_order(where), x, preferred_element_type=F32)
    out[...] = jnp.transpose(rows).astype(BF16)


def regroup(b0, b1, b2, b3, forget, retain):
    for i, b in enumerate((b0, b1, b2, b3)):
        at = i * 16
        forget[at : at + 16, :] = b[0:16, :]
        forget[64 + at : 64 + at + 16, :] = b[16:32, :]
        retain[at : at + 16, :] = b[32:48, :]


def saliency_terms(where, b0, b1, b2, b3, normed_t, grad_y, w_in, w_out, out):
    blocks = (b0, b1, b2, b3)
    act = jnp.concatenate([b[0:64, :] for b in blocks], axis=0)
    grad_pre = jnp.concatenate([b[64:128, :] for b in blocks], axis=0)
    grad_in = jnp.dot(normed_t[...], grad_pre, preferred_element_type=F32)
    grad_out = lax.dot_general(
        act, grad_y[...], (((0,), (0,)), ((), ())), preferred_element_type=F32
    )
    term_in = jnp.sum(jnp.abs(w_in[...].astype(F32) * grad_in), axis=0, keepdims=True)
    prod = jnp.abs(w_out[...].astype(F32) * grad_out)
    lanes = (prod[:, 0:128] + prod[:, 128:256]) + prod[:, 256:384]
    term_out = jnp.sum(jnp.transpose(lanes), axis=0, keepdims=True)
    out[...] = jnp.broadcast_to((term_in + term_out)[None], out.shape)


def retain_product(where, b0, b1, b2, b3, w_out, mine, theirs, acc):
    t = pl.program_id(0)
    act = jnp.concatenate([b0[...], b1[...], b2[...], b3[...]], axis=0)
    part = jnp.dot(act, w_out[...], preferred_element_type=F32)

    @pl.when(t == 0)
    def _():
        acc[...] = part

    @pl.when(t > 0)
    def _():
        acc[...] += part

    def store(swap):
        for j in range(4):
            for i in range(4):
                at = (j * 4 + i) * 16
                to = (i * 4 + j if swap else j * 4 + i) * 8
                mine[to : to + 8, :] = acc[at : at + 8, :]
                theirs[to : to + 8, :] = acc[at + 8 : at + 16, :]

    last = t == pl.num_programs(0) - 1

    @pl.when(last & (where[0] == 0))
    def _():
        store(False)

    @pl.when(last & (where[0] == 1))
    def _():
        store(True)


def call(kernel, where, args, outs, scratch=(), steps=6, vmem=18 * 2**20):
    def spec(shape, block, index):
        if block is None:
            return pl.BlockSpec(shape, lambda t, w: (0,) * len(shape))
        return pl.BlockSpec(block, index)

    return pl.pallas_call(
        kernel,
        grid_spec=pltpu.PrefetchScalarGridSpec(
            num_scalar_prefetch=1,
            grid=(steps,),
            in_specs=[spec(a.shape, b, i) for a, b, i in args],
            out_specs=[spec(s, b, i) for s, _, b, i in outs],
            scratch_shapes=list(scratch),
        ),
        out_shape=[jax.ShapeDtypeStruct(s, d) for s, d, _, _ in outs],
        compiler_params=pltpu.CompilerParams(vmem_limit_bytes=vmem),
        cost_estimate=pl.CostEstimate(flops=1, bytes_accessed=1, transcendentals=0),
    )(where, *[a for a, _, _ in args])


def whole(a):
    return (a, None, None)


def by_n(a, tile=TILE):
    return (a, (a.shape[0], tile), lambda t, w: (0, t))


def out_n(rows, n, dtype, tile=TILE):
    return ((rows, n), dtype, (rows, tile), lambda t, w: (0, t))


def drop_where(kernel):
    def inner(where, *refs):
        kernel(*refs)

    return inner


def permutes(parts, first, sign=1):
    return [
        lax.ppermute(parts[k], ("dp", "col"), pairs(first, sign * (k + 1))) for k in range(3)
    ]


def local(
    forget_tokens,
    forget_cotangent,
    forget_labels,
    retain_tokens,
    ln_gain,
    w_in,
    b_in,
    w_out,
    b_out,
    pruned,
):
    core = lax.axis_index("dp")
    row = lax.axis_index("row")
    col = lax.axis_index("col")
    y, z = col % 4, col // 4
    width = w_in.shape[0]
    half = w_in.shape[1] // 2
    steps = half // TILE
    where = jnp.stack([core, y, z]).astype(jnp.int32)
    gain = ln_gain

    labels = forget_labels[None, :]
    other_f = lax.ppermute(forget_tokens, "dp", SWAP)
    other_r = lax.ppermute(retain_tokens, "dp", SWAP)
    other_g = lax.ppermute(forget_cotangent, "dp", SWAP)
    other_labels = lax.ppermute(labels, "dp", SWAP)

    w_in_tile = (w_in, (width, TILE), lambda t, w: (0, w[0] * steps + t))
    w_out_tile = (w_out, (TILE, width), lambda t, w: (w[0] * steps + t, 0))
    *parts, grad_y, g_part = call(
        partials,
        where,
        [whole(v) for v in (forget_tokens, other_f, forget_cotangent, other_g)]
        + [whole(v) for v in (retain_tokens, other_r, labels, other_labels, gain)]
        + [w_in_tile, w_out_tile],
        [out_n(192, half, BF16)] * 4 + [((256, width), BF16, None, None), out_n(8, half, F32)],
        [pltpu.VMEM((560, width), BF16)],
        steps,
        None,
    )
    got = permutes(parts[1:], True)

    tokens = jnp.stack([forget_tokens, retain_tokens, other_f, other_r])
    tokens, _ = lax.optimization_barrier((tokens, parts[0]))
    tokens = tokens.astype(F32)
    part_mean = jnp.sum(tokens, axis=2) / width
    centred = tokens - part_mean[..., None]
    part_m2 = jnp.sum(centred * centred, axis=2)
    share = jnp.concatenate([part_mean, part_m2, g_part[0].reshape(half // 128, 128)])
    share = jnp.broadcast_to(share[None], (16,) + share.shape)
    share = lax.all_to_all(share, "col", 0, 0, tiled=True)
    b_half = lax.dynamic_slice_in_dim(b_in, core * half, half, 0)[None, :]
    ids = row * w_in.shape[1] + core * half + jnp.arange(half, dtype=jnp.int32)
    is_pruned = jnp.any(pruned[:, None] == ids[None, :], axis=0)
    keep = jnp.where(is_pruned, 0.0, 1.0)[None, :]

    def wide(kernel, args, outs, extra=(), vmem=SMALL):
        return call(
            drop_where(kernel),
            where,
            [by_n(v, WIDE) for v in args] + [whole(v) for v in extra],
            [out_n(rows, half, kind, WIDE) for rows, kind in outs],
            steps=half // WIDE,
            vmem=vmem,
        )

    sums = wide(stage_sum, [parts[0]] + got, [(48, F32)] + [(48, BF16)] * 3)
    back = permutes(sums[1:], False)
    block = call(
        functools.partial(activate, width),
        where,
        [by_n(v, WIDE) for v in [sums[0]] + back + [b_half, keep]] + [whole(share)],
        [out_n(48, half, BF16, WIDE)],
        steps=half // WIDE,
    )[0]
    near = permutes([block] * 3, False, -1)
    share, _ = lax.optimization_barrier((share, block))
    normed_t = call(
        functools.partial(normalise, width),
        where,
        [whole(forget_tokens), whole(other_f), whole(share), whole(gain)],
        [((width, 256), BF16, None, None)],
        (),
        1,
    )[0]
    near[0], normed_t = lax.optimization_barrier((near[0], normed_t))
    forget, retain = wide(regroup, [block] + near, [(128, BF16), (64, BF16)])
    far = permutes([forget] * 3, True, -1)
    first, last, _ = lax.optimization_barrier((w_in, w_out, forget))
    first = lax.dynamic_slice_in_dim(first, core * half, half, 1)
    last = lax.dynamic_slice_in_dim(last, core * half, half, 0)
    retain, first = lax.optimization_barrier((retain, first))
    second, last = lax.optimization_barrier((retain, last))
    far[0], first, last = lax.optimization_barrier((far[0], first, last))
    w_in_tile = (first, (width, TILE), lambda t, w: (0, t))
    w_out_tile = (last, (TILE, width), lambda t, w: (t, 0))
    retain_far = permutes([retain, second, second], True, -1)

    terms = call(
        saliency_terms,
        where,
        [by_n(v) for v in [forget] + far] + [whole(normed_t), whole(grad_y), w_in_tile, w_out_tile],
        [((32, 1, half), F32, (32, 1, TILE), lambda t, w: (0, 0, t))],
        (),
        steps,
    )[0]
    retain_far[0], _ = lax.optimization_barrier((retain_far[0], terms))
    terms = lax.all_to_all(terms, ("dp", "col"), 0, 0, tiled=True)

    mine, theirs = call(
        retain_product,
        where,
        [by_n(v) for v in [retain] + retain_far] + [w_out_tile],
        [((128, width), F32, None, None)] * 2,
        [pltpu.VMEM((256, width), F32)],
        steps,
    )
    mine = (mine + lax.ppermute(theirs, "dp", SWAP)).reshape(4, 4, 8, width)

    def for_row(r):
        return lax.dynamic_index_in_dim(mine, (r - y) % 4, 0, keepdims=False)

    from_rows = [lax.ppermute(for_row(row + k), "row", shift_row(k)) for k in (1, 2, 3)]
    terms, _ = lax.optimization_barrier((terms, from_rows[0]))
    saliency = jnp.sum(terms.reshape(2, 16, half), axis=1).reshape(2 * half) / D
    from_rows[1], saliency = lax.optimization_barrier((from_rows[1], saliency))
    total = for_row(row)
    for part in from_rows:
        total = total + part
    retain_out = (total + b_out).astype(BF16)
    retain_out = lax.dynamic_slice_in_dim(
        jnp.concatenate([retain_out, retain_out], axis=0), (4 - z) % 4, 4, 0
    ).reshape(32, width)
    return (saliency, retain_out)


def solution(mesh):
    in_specs = (
        P("dp", "col"),
        P("dp", "col"),
        P("dp"),
        P("dp", "col"),
        P("col"),
        P("col", "row"),
        P("row"),
        P("row", "col"),
        P("col"),
        P("row"),
    )
    out_specs = (P("row"), P(("dp", "row"), "col"))
    return jax.shard_map(local, mesh=mesh, in_specs=in_specs, out_specs=out_specs, check_vma=False)
```
